256 devices in a mesh: dp: 16 (over x, y), expert: 16 (over z, core).
Axes of the slice: x: 4, y: 4, z: 8, core: 2. Of those that a mesh axis runs over, the one named last changes fastest.
Arguments:
- item_feats: bfloat16 [16, 8192, 256], P('expert', 'dp'), may hold values from -6 to 6
- expert_ids: int32 [16, 8192, 1], P('expert', 'dp'), may hold values from 0 to 63; in each aligned block of 512 rows (0 to 511, 512 to 1023, ..., all dimensions but the last counted through in order) at most 32 rows name the same one
- weight_in: bfloat16 [64, 256, 1024], P('expert'), may hold values from -0.375 to 0.375
- weight_out: bfloat16 [64, 1024, 256], P('expert'), may hold values from -0.1875 to 0.1875
- queries: bfloat16 [16, 8192, 256], P('expert', 'dp'), may hold values from -150 to 150
- query_weight: float32 [16, 8192], P('expert', 'dp'), may hold values from 0.25 to 2
- positives: int32 [16, 8192], P('expert', 'dp'), may hold values from 0 to 8191
- sample_counts: int32 [16, 8192], P('expert'), may hold values from 1 to 4095
Outputs:
- query_loss: float32 [16, 8192], P('expert', 'dp')
- grad_queries: float32 [16, 8192, 256], P('expert', 'dp')
- grad_items: float32 [16, 8192, 256], P('expert', 'dp')
- grad_weight_in: float32 [256, 64, 1024], P('dp', 'expert')
- grad_weight_out: float32 [1024, 64, 256], P('dp', 'expert')
The draws below stay inside these ranges and needn't reach their ends.
Inputs may be any that keep to these rules, and one draw needn't show every extreme that they name: `expert_ids`: the 512 items of one device name each expert at most 32 times.
All inputs are finite; a program needn't handle non-finite values.
Results may differ from the reference program's by a relative error of at most 0.023.
The reference program's roundings to bfloat16 on the way count: a program that leaves them out, or rounds other values in their place, can miss the bound.
Values may be sent and summed in bfloat16 or wider, within the bound.
A program may use at most 128 MiB of HBM per device.

```python
import math
import jax
import jax.numpy as jnp
import numpy as np
from jax import lax

D = 256
FF = 1024
ITEM_DEV = 512
EXPERTS = 64
CAP = 32
POOLS = 16
POOL_ITEMS = 8192
POOL_Q = 8192
N_DP = 16


def draw_queries(key, part):
    normal_values = jax.random.normal(key, (POOLS, POOL_Q, D), jnp.float32) * 3.0
    return jnp.clip(normal_values, -18.0, 18.0).astype(jnp.bfloat16)


def with_ends(values, stream_key, smallest, top_value):
    shape = values.shape
    place = [jax.random.randint(jax.random.fold_in(stream_key, axis), (), 0, shape[axis]) for axis in range(len(shape))]
    values = values.at[tuple(place)].set(smallest)
    longest = shape.index(max(shape))
    place[longest] = (place[longest] + 1) % shape[longest]
    return values.at[tuple(place)].set(top_value)


def steps_of(stream_key, extent, cuts, low, top_value):
    def one(axis_at, blocks):
        draws = jax.random.uniform(jax.random.fold_in(jax.random.fold_in(stream_key, 6), axis_at), (blocks,), jnp.float32, low / len(cuts), top_value / len(cuts))
        return jnp.repeat(jnp.exp(draws), extent[axis_at] // blocks).reshape((-1,) + (1,) * (len(extent) - axis_at - 1))

    gain = one(*cuts[0])
    for cut in cuts[1:]:
        gain = gain * one(*cut)
    return gain


def assign_block(rng, own, number, rows, number_of, top, bound, slope):
    order = jax.random.permutation(rng, number_of)
    heavy_load, ordinary = shares(number_of, rows * top, bound, slope, True), shares(number_of, rows * top, bound, slope, False)
    places = jnp.arange(number_of)

    def named(sizes, offset_by):
        used = int((sizes > 0).sum())
        fixed = max(1, used // 4)
        shifted = fixed + (places - fixed + offset_by * (used - fixed)) % max(1, number_of - fixed)
        return jnp.zeros((number_of,), jnp.int32).at[order[jnp.where(places < fixed, places, shifted)]].set(jnp.asarray(sizes, jnp.int32))

    sizes = jnp.where(number % 4 == 0, named(heavy_load, number // 4), named(ordinary, number - number // 4 - 1))
    mixed = jax.random.permutation(jax.random.fold_in(own, 3), number_of)
    donor, receiver = mixed[0:number_of // 2 * 2:2], mixed[1:number_of // 2 * 2:2]
    slack = jnp.minimum(sizes[donor] - 1, bound - sizes[receiver]) // 2
    slack = jnp.where((donor == order[0]) | (receiver == order[0]) | (sizes[receiver] == 0), 0, jnp.maximum(slack, 0))
    shifted = jax.random.randint(jax.random.fold_in(own, 4), (number_of // 2,), 0, 1 << 20) % (slack + 1)
    sizes = sizes.at[donor].add(-shifted).at[receiver].add(shifted)
    items = jnp.searchsorted(jnp.cumsum(sizes), jnp.arange(rows * top), side="right").astype(jnp.int32)
    table = items.reshape(top, rows).T
    table = table[jax.random.permutation(jax.random.fold_in(own, 1), rows)]
    offset_by = jax.random.randint(jax.random.fold_in(own, 2), (rows, 1), 0, top)
    return jnp.take_along_axis(table, (jnp.arange(top)[None, :] + offset_by) % top, axis=1)


def shares(number_of, total, limit, slope, full):
    weights = [(1 << 20) // math.isqrt(standing ** slope) + 1 for standing in range(1, number_of + 1)]
    largest = limit if full else min(limit, max(-(-total // number_of), total * weights[0] // sum(weights)))
    least = 1 if total - largest >= number_of - 1 else 0
    given, rest = [largest] + [least] * (number_of - 1), total - largest - least * (number_of - 1)
    while rest > 0:
        free = [i for i in range(1, number_of) if given[i] < largest] or [i for i in range(1, number_of) if given[i] < limit]
        mass, budget = sum([weights[i] for i in free]), rest
        for i in free:
            extra = min(limit - given[i], max(1, budget * weights[i] // mass), rest)
            given[i] = given[i] + extra
            rest = rest - extra
    return np.array(given)


def centred(key, extent, deviation, limit, split=(), held_as=jnp.bfloat16):
    array = jax.random.normal(key, extent, jnp.float32) * deviation
    if len(split) > 0:
        array = steps_of(key, extent, split, -0.22, 0.18) * array
    return jnp.clip(array, min=-limit, max=limit).astype(held_as)


def setup_inputs(seed: int = 0) -> dict:
    arg_keys = jax.random.split(jax.random.key(seed), 9)
    item_feats = centred(arg_keys[0], (POOLS, POOL_ITEMS, D), 1.0, 6.0, ((0, 16), (1, 16)))
    expert_ids_keys = jax.random.split(jax.random.fold_in(arg_keys[1], 1), POOLS * POOL_ITEMS // ITEM_DEV)
    expert_ids_turns = jax.random.permutation(jax.random.fold_in(arg_keys[1], 3), POOLS * POOL_ITEMS // ITEM_DEV)
    expert_ids = jax.vmap(lambda own, number: assign_block(jax.random.fold_in(arg_keys[1], 2), own, number, ITEM_DEV, EXPERTS, 1, CAP, 2))(expert_ids_keys, expert_ids_turns).reshape((POOLS, POOL_ITEMS, 1))
    weight_in = centred(arg_keys[2], (EXPERTS, D, FF), D ** -0.5, 0.375, ((0, 16),))
    weight_out = centred(arg_keys[3], (EXPERTS, FF, D), FF ** -0.5, 0.1875, ((0, 16),))
    queries = draw_queries(jax.random.fold_in(arg_keys[8], 71), 0)
    query_weight = jnp.clip(jnp.exp(math.log(2.0) - 2.0794415 * jax.random.uniform(arg_keys[5], (POOLS, POOL_Q), jnp.float32) ** steps_of(arg_keys[5], (POOLS, POOL_Q), ((0, 16), (1, 16)), -0.2, 0.2)), 0.25, 2.0)
    positives = with_ends(jax.random.randint(arg_keys[6], (POOLS, POOL_Q), 0, POOL_ITEMS), jax.random.fold_in(arg_keys[6], 1), 0, POOL_ITEMS - 1).astype(jnp.int32)
    sample_counts = with_ends(jax.random.randint(arg_keys[7], (POOLS, POOL_ITEMS), 1, 4096), jax.random.fold_in(arg_keys[7], 1), 1, 4095).astype(jnp.int32)
    return dict(item_feats=item_feats, expert_ids=expert_ids, weight_in=weight_in, weight_out=weight_out, queries=queries, query_weight=query_weight, positives=positives, sample_counts=sample_counts)


norm_eps = 1e-06
block_rows = 64

def arrange(routes):
    labels = jnp.arange(EXPERTS, dtype=jnp.int32)
    onehot = (routes[:, None] == labels[None, :]).astype(jnp.int32)
    expert_loads = lax.optimization_barrier(jnp.sum(onehot, axis=0)).astype(jnp.int32)
    padded_rows = ((expert_loads + block_rows - 1) // block_rows * block_rows).astype(jnp.int32)
    range_ends = jnp.cumsum(padded_rows).astype(jnp.int32)
    starts = (range_ends - padded_rows).astype(jnp.int32)
    before = (jnp.cumsum(onehot, axis=0).astype(jnp.int32) - onehot).astype(jnp.int32)
    places = lax.optimization_barrier(jnp.sum(onehot * (before + starts[None, :]), axis=1)).astype(jnp.int32)
    blocks = (routes.shape[0] + block_rows - 1) // block_rows + EXPERTS
    firsts = jnp.arange(blocks, dtype=jnp.int32) * block_rows
    owners = lax.optimization_barrier(jnp.sum((range_ends[None, :] <= firsts[:, None]).astype(jnp.int32), axis=1))
    owners = jnp.minimum(owners, EXPERTS - 1).astype(jnp.int32)
    return (places, owners, blocks)

def rows_of(source, row_index):
    picked = lax.dynamic_slice_in_dim(source, (row_index * ITEM_DEV).astype(jnp.int32), ITEM_DEV, 1)
    return picked.reshape((POOLS * ITEM_DEV,) + source.shape[2:])

def unrows(stacked):
    shaped = stacked.reshape((N_DP, POOLS, ITEM_DEV) + stacked.shape[2:])
    return jnp.moveaxis(shaped, 0, 1).reshape((POOLS, POOL_ITEMS) + stacked.shape[2:])

def pool_half(inputs):
    pool_queries, pool_units, pool_logs, pool_weights, pool_targets = inputs
    query_block = math.gcd(POOL_Q, 1024)
    block_tally = POOL_Q // query_block
    columns = jnp.arange(POOL_ITEMS, dtype=jnp.int32)

    def query_part(parts):
        block_queries, block_weights, block_targets = parts
        scores = jnp.dot(block_queries, pool_units.T, preferred_element_type=jnp.float32) - pool_logs[None, :]
        highest = lax.optimization_barrier(jnp.max(scores, axis=1, keepdims=True))
        log_total = highest[:, 0] + jnp.log(lax.optimization_barrier(jnp.sum(jnp.exp(scores - highest), axis=1)))
        target_hit = columns[None, :] == block_targets[:, None]
        picked = lax.optimization_barrier(jnp.sum(jnp.where(target_hit, scores, 0.0), axis=1))
        mixing_factors = (block_weights[:, None] * (jnp.exp(scores - log_total[:, None]) - target_hit.astype(jnp.float32))).astype(jnp.bfloat16)
        grad_query = jnp.dot(mixing_factors, pool_units, preferred_element_type=jnp.float32)
        grad_unit = jnp.dot(mixing_factors.T, block_queries, preferred_element_type=jnp.float32)
        return (log_total - picked, grad_query, grad_unit)
    losses, grad_query, grad_unit = lax.map(query_part, (pool_queries.reshape(block_tally, query_block, D), pool_weights.reshape(block_tally, query_block), pool_targets.reshape(block_tally, query_block)))
    return (losses.reshape(POOL_Q), grad_query.reshape(POOL_Q, D), lax.optimization_barrier(jnp.sum(grad_unit, axis=0)))

def reference(item_feats, expert_ids, weight_in, weight_out, queries, query_weight, positives, sample_counts):
    features = item_feats.astype(jnp.float32)
    inv_rms = lax.rsqrt(lax.optimization_barrier(jnp.mean(features * features, axis=2, keepdims=True)) + norm_eps)
    normed = (features * inv_rms).astype(jnp.bfloat16)
    routes = expert_ids[:, :, 0]

    def forward_row(row_index):
        row_feats = rows_of(normed, row_index)
        places, owners, blocks = arrange(rows_of(routes, row_index))
        slot_rows = jnp.zeros((blocks * block_rows, D), jnp.bfloat16).at[places].set(row_feats).reshape(blocks, block_rows, D)

        def expert_block(parts):
            slot_block, owner_id = parts
            hidden = jnp.dot(slot_block, weight_in[owner_id], preferred_element_type=jnp.float32)
            active = jax.nn.gelu(hidden).astype(jnp.bfloat16)
            return jnp.dot(active, weight_out[owner_id], preferred_element_type=jnp.float32).astype(jnp.bfloat16)
        outputs = lax.map(expert_block, (slot_rows, owners))
        return outputs.reshape(blocks * block_rows, D)[places]
    branch = unrows(lax.map(forward_row, jnp.arange(N_DP, dtype=jnp.int32)))
    reduced_sum = features + branch.astype(jnp.float32)
    length = jnp.sqrt(lax.optimization_barrier(jnp.sum(reduced_sum * reduced_sum, axis=2, keepdims=True)) + norm_eps)
    unit_vecs = reduced_sum / length
    unit_low = unit_vecs.astype(jnp.bfloat16)
    log_counts = jnp.log(sample_counts.astype(jnp.float32))
    query_loss, grad_queries, grad_unit = lax.map(pool_half, (queries, unit_low, log_counts, query_weight, positives))
    along = lax.optimization_barrier(jnp.sum(unit_vecs * grad_unit, axis=2, keepdims=True))
    grad_summed = (grad_unit - unit_vecs * along) / length
    grad_low = grad_summed.astype(jnp.bfloat16)

    def backward_row(totals, row_index):
        total_in, total_out = totals
        row_feats = rows_of(normed, row_index)
        row_grads = rows_of(grad_low, row_index)
        places, owners, blocks = arrange(rows_of(routes, row_index))
        slot_feats = jnp.zeros((blocks * block_rows, D), jnp.bfloat16).at[places].set(row_feats).reshape(blocks, block_rows, D)
        slot_grads = jnp.zeros((blocks * block_rows, D), jnp.bfloat16).at[places].set(row_grads).reshape(blocks, block_rows, D)

        def expert_block(sums, parts):
            sum_in, sum_out = sums
            block_feats, block_grads, owner_id = parts
            hidden = jnp.dot(block_feats, weight_in[owner_id], preferred_element_type=jnp.float32)
            active = jax.nn.gelu(hidden).astype(jnp.bfloat16)
            grad_active = jnp.dot(block_grads, weight_out[owner_id].T, preferred_element_type=jnp.float32)
            grad_hidden = jax.vjp(jax.nn.gelu, hidden)[1](grad_active)[0].astype(jnp.bfloat16)
            grad_normed = jnp.dot(grad_hidden, weight_in[owner_id].T, preferred_element_type=jnp.float32).astype(jnp.bfloat16)
            sum_in = sum_in.at[owner_id].add(jnp.dot(block_feats.T, grad_hidden, preferred_element_type=jnp.float32))
            sum_out = sum_out.at[owner_id].add(jnp.dot(active.T, block_grads, preferred_element_type=jnp.float32))
            return ((sum_in, sum_out), grad_normed)
        start_sums = (jnp.zeros((EXPERTS, D, FF), jnp.float32), jnp.zeros((EXPERTS, FF, D), jnp.float32))
        (sum_in, sum_out), grad_normed = lax.scan(expert_block, start_sums, (slot_feats, slot_grads, owners))
        rounded_in = lax.optimization_barrier(sum_in.astype(jnp.bfloat16))
        rounded_out = lax.optimization_barrier(sum_out.astype(jnp.bfloat16))
        totals = (total_in + rounded_in.astype(jnp.float32), total_out + rounded_out.astype(jnp.float32))
        return (totals, grad_normed.reshape(blocks * block_rows, D)[places])
    start_totals = (jnp.zeros((EXPERTS, D, FF), jnp.float32), jnp.zeros((EXPERTS, FF, D), jnp.float32))
    (total_in, total_out), grad_stack = lax.scan(backward_row, start_totals, jnp.arange(N_DP, dtype=jnp.int32))
    grad_rows = unrows(grad_stack).astype(jnp.float32)
    projected = lax.optimization_barrier(jnp.mean(grad_rows * features, axis=2, keepdims=True))
    grad_items = grad_summed + inv_rms * (grad_rows - features * inv_rms * inv_rms * projected)
    return (query_loss, grad_queries, grad_items, jnp.transpose(total_in, (1, 0, 2)), jnp.transpose(total_out, (1, 0, 2)))
```

```python
import functools
import math

import jax
import jax.numpy as jnp
from jax import lax
from jax.experimental import pallas as pl
from jax.experimental.pallas import tpu as pltpu
from jax.sharding import Mesh
from jax.sharding import PartitionSpec as P

AXES = ("x", "y", "z", "c")
SIZE = {"x": 4, "y": 4, "z": 8, "c": 2}
N = 512
D = 256
FF = 1024
NE = 4
CAP = 32
EXPERTS = 64
GROUP = 16
SLOTS = NE * CAP
EPS = 1e-6
K0 = math.sqrt(2.0 / math.pi)
K1 = K0 * 0.044715
BF = jnp.bfloat16
F32 = jnp.float32

DZ = (0, 1, 7, 2, 6, 3, 5, 4)


def at(axis, step):
    return lax.rem(lax.axis_index(axis) + (step % SIZE[axis]), SIZE[axis])


def z_peer(p, sign):
    return {"z": at("z", sign * DZ[p // 2]), "c": at("c", p % 2)}


def xy_peer(j):
    return {"x": at("x", j // 4), "y": at("y", j % 4)}


def nt(a, b):
    return lax.dot_general(a, b, (((1,), (1,)), ((), ())), preferred_element_type=F32)


def nn(a, b):
    return jnp.dot(a, b, preferred_element_type=F32)


def remote(src, dst, send, recv, peer):
    return pltpu.make_async_remote_copy(
        src_ref=src, dst_ref=dst, send_sem=send, recv_sem=recv, device_id=peer
    )


class RingGather:
    def __init__(self, buf, send, recv):
        self.buf, self.send, self.recv = buf, send, recv
        self.copies = {}

    def go(self, number, view, peer):
        c = remote(view, view, self.send.at[number], self.recv.at[number], peer)
        c.start()
        self.copies[number] = c

    def got(self, *numbers):
        for n in numbers:
            self.copies[n].wait_recv()

    def step(self, s):
        buf, h, q = self.buf, N // 2, N // 4
        x, y = lax.axis_index("x"), lax.axis_index("y")
        xl, xr, yl, yr = at("x", -1), at("x", 1), at("y", -1), at("y", 1)
        top, bot = pl.ds(0, h), pl.ds(h, h)
        parts = [pl.ds(i * q, q) for i in range(4)]
        if s == 0:
            self.go(0, buf.at[x, y, top], {"x": xr})
            self.go(1, buf.at[x, y, top], {"x": xl})
            self.go(2, buf.at[x, y, bot], {"y": yr})
            self.go(3, buf.at[x, y, bot], {"y": yl})
        elif s == 1:
            self.got(0, 1, 2, 3)
            self.go(4, buf.at[xl, y, parts[0]], {"x": xr})
            self.go(5, buf.at[xr, y, parts[1]], {"x": xl})
            self.go(6, buf.at[x, yl, parts[2]], {"y": yr})
            self.go(7, buf.at[x, yr, parts[3]], {"y": yl})
        elif s == 2:
            self.got(4, 5, 6, 7)
            self.go(8, buf.at[:, y, top], {"y": yr})
            self.go(9, buf.at[:, y, top], {"y": yl})
            self.go(10, buf.at[x, :, bot], {"x": xr})
            self.go(11, buf.at[x, :, bot], {"x": xl})
        elif s == 3:
            self.got(8, 9, 10, 11)
            self.go(12, buf.at[:, yl, parts[0]], {"y": yr})
            self.go(13, buf.at[:, yr, parts[1]], {"y": yl})
            self.go(14, buf.at[xl, :, parts[2]], {"x": xr})
            self.go(15, buf.at[xr, :, parts[3]], {"x": xl})
        else:
            self.got(12, 13, 14, 15)
            for c in self.copies.values():
                c.wait_send()


def kernel(
    feats, ids_col, ids_row, w_in_hbm, w_out_hbm, queries, qw_row, pos_row, qw_col, pos_col, logc_col, logc_all,
    loss_o, gq_o, gi_o, gwi_o, gwo_o,
    w_in, w_out, q_all, u_all, nrm, ulow, unit, invlen, gs, acc, lb, plr, plc,
    snd, rcv, outb, ret, gsnd, grcv, gnb, gnret,
    gp, act_t, x_t, gh, pin, pout, ra_in, ra_out, pa_in, pa_out, rb_in, rb_out,
    st_s, st_r, bc_s, bc_r,
    loc_sem, a1s, a1r, a2s, a2r, a3s, a3r, a4s, a4r, qs, qr, us, ur, sts, str_, bcs, bcr, rs_s, rs_r,
):
    x, y, z, c = (lax.axis_index(a) for a in AXES)
    barrier = pltpu.get_barrier_semaphore()
    for p in range(1, GROUP):
        pl.semaphore_signal(barrier, inc=1, device_id=z_peer(p, 1))
    for j in range(1, GROUP):
        pl.semaphore_signal(barrier, inc=1, device_id=xy_peer(j))

    load_in = pltpu.make_async_copy(w_in_hbm, w_in, loc_sem.at[0])
    load_out = pltpu.make_async_copy(w_out_hbm, w_out, loc_sem.at[1])
    load_in.start()
    load_out.start()
    q_all[x, y] = queries[...]

    def place(ids, rank):
        owner = ids >> 2
        dz = ((owner >> 1) - z) & 7
        dc = ((owner & 1) - c) & 1
        pz = jnp.where(dz <= 4, jnp.maximum(2 * dz - 1, 0), 16 - 2 * dz)
        return (pz * 2 + dc) * SLOTS + (ids & 3) * CAP + rank

    f = feats[...].astype(F32)
    r = lax.rsqrt(jnp.mean(f * f, axis=1, keepdims=True) + EPS)
    nrm[...] = (f * r).astype(BF)
    row_i = lax.broadcasted_iota(jnp.int32, (N, N), 0)
    col_i = lax.broadcasted_iota(jnp.int32, (N, N), 1)
    idr = ids_row[...]
    hot_r = lax.broadcasted_iota(jnp.int32, (EXPERTS, N), 0) == idr
    before = nn(hot_r.astype(F32).astype(BF), (row_i < col_i).astype(F32).astype(BF))
    rank_r = jnp.sum(jnp.where(hot_r, before, 0.0), axis=0, keepdims=True)
    plr[...] = place(idr, rank_r.astype(jnp.int32))
    idc = ids_col[...]
    hot_c = lax.broadcasted_iota(jnp.int32, (N, EXPERTS), 1) == idc
    before = nn((row_i > col_i).astype(F32).astype(BF), hot_c.astype(F32).astype(BF))
    rank_c = jnp.sum(jnp.where(hot_c, before, 0.0), axis=1, keepdims=True)
    plc[...] = jnp.broadcast_to(place(idc, rank_c.astype(jnp.int32)), (N, 2 * SLOTS))
    lb[...] = jnp.broadcast_to(logc_col[...], (N, D))

    def packed(values, p):
        slot = lax.broadcasted_iota(jnp.int32, (SLOTS, N), 0) + p * SLOTS
        pick = (slot == plr[...]).astype(F32).astype(BF)
        return nn(pick, values[...]).astype(BF).reshape(NE, CAP, D)

    def unpacked(source, i):
        slot = lax.broadcasted_iota(jnp.int32, (N, 2 * SLOTS), 1) + i * 2 * SLOTS
        pick = (slot == plc[...]).astype(F32).astype(BF)
        return nn(pick, source[pl.ds(2 * i, 2)].reshape(2 * SLOTS, D))

    pl.semaphore_wait(barrier, 2 * (GROUP - 1))
    gather_q = RingGather(q_all, qs, qr)
    gather_q.step(0)

    def dispatch(values, out, into, send, recv):
        copies = {}
        for p in range(GROUP):
            if p == 0:
                into[0] = packed(values, 0)
            else:
                out[p] = packed(values, p)
                copies[p] = remote(out.at[p], into.at[p], send.at[p], recv.at[p], z_peer(p, 1))
                copies[p].start()
        return copies

    def give_back(out, into, send, recv, p):
        copy = remote(out.at[p], into.at[p], send.at[p], recv.at[p], z_peer(p, -1))
        copy.start()
        return copy

    sent1 = dispatch(nrm, snd, rcv, a1s, a1r)
    load_in.wait()
    load_out.wait()
    gather_q.step(1)

    back2 = {}
    for b in range(4):
        for p in range(4 * b, 4 * b + 4):
            if p:
                sent1[p].wait_recv()

        def forward(e, _, b=b):
            rows = rcv[pl.ds(4 * b, 4), e].reshape(4 * CAP, D)
            h = nn(rows, w_in[e])
            gp[b, e] = h
            t = jnp.tanh(h * (K0 + K1 * (h * h)))
            act = (h * (0.5 + 0.5 * t)).astype(BF)
            out = nn(act, w_out[e]).astype(BF)
            outb[pl.ds(4 * b, 4), e] = out.reshape(4, CAP, D)
            return _

        lax.fori_loop(0, NE, forward, 0)
        for p in range(4 * b, 4 * b + 4):
            if p:
                back2[p] = give_back(outb, ret, a2s, a2r, p)
        if b == 0:
            ret[0] = outb[0]
        if b < 3:
            gather_q.step(2 + b)

    for b in range(4):

        def keep(e, _, b=b):
            h = gp[b, e]
            u = h * h
            t = jnp.tanh(h * (K0 + K1 * u))
            cdf = 0.5 + 0.5 * t
            act = (h * cdf).astype(BF)
            gp[b, e] = cdf + (0.5 * h) * (1.0 - t * t) * (K0 + (3.0 * K1) * u)
            act_t[e, :, pl.ds(4 * CAP * b, 4 * CAP)] = act.T
            rows = rcv[pl.ds(4 * b, 4), e].reshape(4 * CAP, D)
            x_t[e, :, pl.ds(4 * CAP * b, 4 * CAP)] = rows.T
            return _

        lax.fori_loop(0, NE, keep, 0)

    acc[...] = jnp.zeros((N, D), F32)
    for i in range(8):
        for p in (2 * i, 2 * i + 1):
            if p:
                back2[p].wait_recv()
        acc[...] += unpacked(ret, i)

    summed = feats[...].astype(F32) + acc[...]
    length = jnp.sqrt(jnp.sum(summed * summed, axis=1, keepdims=True) + EPS)
    inv = 1.0 / length
    un = summed * inv
    unit[...] = un
    invlen[...] = jnp.broadcast_to(inv, (N, 128))
    ulow[...] = un.astype(BF)
    u_all[x, y] = un.astype(BF)
    gather_u = RingGather(u_all, us, ur)
    gather_u.step(0)

    T = 256

    def scores(qx, qy, t):
        return nt(ulow[...], q_all[qx, qy, pl.ds(t * T, T)]) - lb[...]

    def stat_block(j, _):
        qx, qy = lax.rem(x + j // 4, 4), lax.rem(y + lax.rem(j, 4), 4)
        for t in range(N // T):
            s = scores(qx, qy, t)
            m = jnp.max(s, axis=0, keepdims=True)
            st_s[j, 0:1, pl.ds(t * T, T)] = m
            st_s[j, 1:2, pl.ds(t * T, T)] = jnp.sum(jnp.exp(s - m), axis=0, keepdims=True)
        return _

    st_copies = {}
    for part in range(4):
        lax.fori_loop(4 * part, 4 * part + 4, stat_block, 0)
        for j in range(4 * part, 4 * part + 4):
            if j:
                st_copies[j] = remote(st_s.at[j], st_r.at[j], sts.at[j], str_.at[j], xy_peer(j))
                st_copies[j].start()
        if part < 3:
            gather_u.step(1 + part)
    st_r[0] = st_s[0]
    for j in range(1, GROUP):
        st_copies[j].wait_recv()
    top = jnp.max(st_r[:, 0:1, :], axis=0)
    total = jnp.sum(st_r[:, 1:2, :] * jnp.exp(st_r[:, 0:1, :] - top[None]), axis=0)
    lse = top + jnp.log(total)
    shift = lse - jnp.log(qw_row[...])
    bc_s[0:1] = shift
    bc_s[1:2] = qw_row[...]
    bc_s[2:3] = pos_row[...].astype(F32)
    bc_s[3:4] = lse
    bc_copies = {}
    for j in range(1, GROUP):
        bc_copies[j] = remote(bc_s, bc_r.at[j], bcs.at[j], bcr.at[j], xy_peer(j))
        bc_copies[j].start()
    bc_r[0] = bc_s[...]
    first_item = ((x * 4 + y) * N).astype(F32)

    acc[...] = jnp.zeros((N, D), F32)
    item_row = lax.broadcasted_iota(jnp.int32, (N, T), 0)

    def grad_block(j, _):
        qx, qy = lax.rem(x + 4 - j // 4, 4), lax.rem(y + 4 - lax.rem(j, 4), 4)
        for t in range(N // T):
            span = pl.ds(t * T, T)
            s = scores(qx, qy, t)
            e = jnp.exp(s - bc_r[j, 0:1, span])
            own = (bc_r[j, 2:3, span] - first_item).astype(jnp.int32)
            coeff = (e - jnp.where(item_row == own, bc_r[j, 1:2, span], 0.0)).astype(BF)
            acc[...] += nn(coeff, q_all[qx, qy, span])
        return _

    for part in range(4):
        for j in range(4 * part, 4 * part + 4):
            if j:
                bc_copies[j].wait_recv()
        lax.fori_loop(4 * part, 4 * part + 4, grad_block, 0)

    g = acc[...]
    un = unit[...]
    along = jnp.sum(un * g, axis=1, keepdims=True)
    gsum = (g - un * along) * invlen[:, 0:1]
    gs[...] = gsum
    nrm[...] = gsum.astype(BF)
    sent3 = dispatch(nrm, gsnd, grcv, a3s, a3r)
    gather_u.step(4)

    acc[...] = jnp.zeros((N, D), F32)
    lse_c = jnp.transpose(jnp.broadcast_to(lse, (8, N)))[:, 0:1]
    shift_c = lse_c - jnp.log(qw_col[...])
    lb[...] = jnp.broadcast_to(shift_c, (N, D))
    plq = jnp.broadcast_to(pos_col[...], (N, 128))
    invlen[...] = jnp.zeros((N, 128), F32)

    def query_block(d, _):
        ix, iy = d // 4, lax.rem(d, 4)
        for t in range(N // 128):
            span = pl.ds(t * 128, 128)
            s = nt(queries[...], u_all[ix, iy, span]) - logc_all[d, 0:1, span]
            e = jnp.exp(s - lb[:, 0:128])
            hit = lax.broadcasted_iota(jnp.int32, (N, 128), 1) + (d * N + t * 128) == plq
            coeff = (e - jnp.where(hit, jnp.broadcast_to(qw_col[...], (N, 128)), 0.0)).astype(BF)
            invlen[...] += jnp.where(hit, s, 0.0)
            acc[...] += nn(coeff, u_all[ix, iy, span])
        return _

    lax.fori_loop(0, GROUP, query_block, 0)
    gq_o[...] = acc[...]
    picked = jnp.sum(invlen[...], axis=1, keepdims=True)
    loss_c = jnp.broadcast_to(lse_c - picked, (N, 128))
    loss_o[...] = jnp.transpose(loss_c)[0:1]

    back4 = {}
    for b in range(4):
        for p in range(4 * b, 4 * b + 4):
            if p:
                sent3[p].wait_recv()

        def backward(e, _, b=b):
            rows = grcv[pl.ds(4 * b, 4), e].reshape(4 * CAP, D)
            ga = nt(rows, w_out[e])
            ghv = (ga * gp[b, e]).astype(BF)
            gh[e, pl.ds(4 * CAP * b, 4 * CAP)] = ghv
            gnb[pl.ds(4 * b, 4), e] = nt(ghv, w_in[e]).astype(BF).reshape(4, CAP, D)
            return _

        lax.fori_loop(0, NE, backward, 0)
        for p in range(4 * b, 4 * b + 4):
            if p:
                back4[p] = give_back(gnb, gnret, a4s, a4r, p)
        if b == 0:
            gnret[0] = gnb[0]

    def weights(e, _):
        pin[:, :, e] = nn(x_t[e], gh[e]).astype(BF).reshape(4, 4, 16, FF)
        rows = grcv[:, e].reshape(GROUP * CAP, D)
        pout[:, :, e] = nn(act_t[e], rows).astype(BF).reshape(4, 4, 64, D)
        return _

    lax.fori_loop(0, NE, weights, 0)

    rs = {}

    def rs_go(number, src, dst, peer):
        rs[number] = remote(src, dst, rs_s.at[number], rs_r.at[number], peer)
        rs[number].start()

    for k in (1, 3, 2):
        rs_go(k - 1, pin.at[at("x", k)], ra_in.at[k - 1], {"x": at("x", k)})
        rs_go(k + 2, pout.at[:, at("y", k)], ra_out.at[k - 1], {"y": at("y", k)})

    acc[...] = jnp.zeros((N, D), F32)
    for i in range(8):
        for p in (2 * i, 2 * i + 1):
            if p:
                back4[p].wait_recv()
        acc[...] += unpacked(gnret, i)
    f = feats[...].astype(F32)
    r = lax.rsqrt(jnp.mean(f * f, axis=1, keepdims=True) + EPS)
    grows = acc[...]
    projected = jnp.mean(grows * f, axis=1, keepdims=True)
    gi_o[...] = gs[...] + r * (grows - f * (r * r * projected))

    for n in range(6):
        rs[n].wait_recv()
    for k in range(4):
        t = pin[x, k].astype(F32)
        u = pout[k, y].astype(F32)
        for i in range(3):
            t = t + ra_in[i, k].astype(F32)
            u = u + ra_out[i, k].astype(F32)
        pa_in[k] = t.astype(BF)
        pa_out[k] = u.astype(BF)
    for k in (1, 3, 2):
        rs_go(k + 5, pa_in.at[at("y", k)], rb_in.at[k - 1], {"y": at("y", k)})
        rs_go(k + 8, pa_out.at[at("x", k)], rb_out.at[k - 1], {"x": at("x", k)})
    for n in range(6, 12):
        rs[n].wait_recv()
    t = pa_in[y].astype(F32)
    u = pa_out[x].astype(F32)
    for i in range(3):
        t = t + rb_in[i].astype(F32)
        u = u + rb_out[i].astype(F32)
    gwi_o[...] = t
    gwo_o[...] = u

    for group in (sent1, back2, sent3, back4, st_copies, bc_copies, rs):
        for copy in group.values():
            copy.wait_send()


def per_device(feats, ids, w_in, w_out, queries, qw, pos, counts):
    d = lax.axis_index("x") * 4 + lax.axis_index("y")
    logc = jnp.log(counts[0].astype(F32)).reshape(GROUP, 1, N)
    own = lax.dynamic_index_in_dim(logc, d, 0, keepdims=False).reshape(N, 1)
    vm = pl.BlockSpec(memory_space=pltpu.VMEM)
    hbm = pl.BlockSpec(memory_space=pl.ANY)
    V = pltpu.VMEM
    sem = pltpu.SemaphoreType.DMA
    slots = (GROUP, NE, CAP, D)
    scratch = [
        V((NE, D, FF), BF), V((NE, FF, D), BF), V((4, 4, N, D), BF), V((4, 4, N, D), BF),
        V((N, D), BF), V((N, D), BF), V((N, D), F32), V((N, 128), F32), V((N, D), F32), V((N, D), F32), V((N, D), F32),
        V((1, N), jnp.int32), V((N, 2 * SLOTS), jnp.int32),
        *[V(slots, BF) for _ in range(8)],
        V((4, NE, 4 * CAP, FF), F32), V((NE, FF, N), BF), V((NE, D, N), BF), V((NE, N, FF), BF),
        V((4, 4, NE, 16, FF), BF), V((4, 4, NE, 64, D), BF),
        V((3, 4, NE, 16, FF), BF), V((3, 4, NE, 64, D), BF),
        V((4, NE, 16, FF), BF), V((4, NE, 64, D), BF),
        V((3, NE, 16, FF), BF), V((3, NE, 64, D), BF),
        V((GROUP, 2, N), F32), V((GROUP, 2, N), F32), V((4, N), F32), V((GROUP, 4, N), F32),
        sem((2,)), *[sem((GROUP,)) for _ in range(16)], sem((12,)), sem((12,)),
    ]
    outs = (
        jax.ShapeDtypeStruct((1, N), F32),
        jax.ShapeDtypeStruct((N, D), F32),
        jax.ShapeDtypeStruct((N, D), F32),
        jax.ShapeDtypeStruct((NE, 16, FF), F32),
        jax.ShapeDtypeStruct((NE, 64, D), F32),
    )
    loss, gq, gi, gwi, gwo = pl.pallas_call(
        kernel,
        out_shape=outs,
        in_specs=[vm, vm, vm, hbm, hbm, vm, vm, vm, vm, vm, vm, vm],
        out_specs=[vm] * 5,
        scratch_shapes=scratch,
        compiler_params=pltpu.CompilerParams(
            collective_id=0, has_side_effects=True, vmem_limit_bytes=60 << 20
        ),
        name="tower_step",
    )(
        feats[0], ids[0], ids.reshape(1, N), w_in, w_out, queries[0], qw, pos,
        qw.reshape(N, 1), pos.reshape(N, 1), own, logc,
    )
    return (loss, gq[None], gi[None], jnp.transpose(gwi, (1, 0, 2)), jnp.transpose(gwo, (1, 0, 2)))


def solution(mesh):
    torus = Mesh(mesh.devices.reshape(4, 4, 8, 2), AXES)
    dp, ex = ("x", "y"), ("z", "c")
    in_specs = (
        P(ex, dp, None), P(ex, dp, None), P(ex, None, None), P(ex, None, None),
        P(ex, dp, None), P(ex, dp), P(ex, dp), P(ex, None),
    )
    out_specs = (
        P(ex, dp), P(ex, dp, None), P(ex, dp, None), P(dp, ex, None), P(dp, ex, None),
    )
    return jax.shard_map(
        per_device, mesh=torus, in_specs=in_specs, out_specs=out_specs, check_vma=False
    )
```

```python
import functools
import math

import jax
import jax.numpy as jnp
from jax import lax
from jax.experimental import pallas as pl
from jax.experimental.pallas import tpu as pltpu
from jax.sharding import Mesh
from jax.sharding import PartitionSpec as P

AXES = ("x", "y", "z", "c")
SIZE = {"x": 4, "y": 4, "z": 8, "c": 2}
N = 512
D = 256
FF = 1024
NE = 4
CAP = 32
EXPERTS = 64
GROUP = 16
SLOTS = NE * CAP
NG = 2
EG = NE // NG
MSG = EG * CAP
GSLOTS = GROUP * MSG
T = 256
QCUT = 8
PACK = 512
EPS = 1e-6
K0 = math.sqrt(2.0 / math.pi)
K1 = K0 * 0.044715
BF = jnp.bfloat16
F32 = jnp.float32

DZ = (0, 1, 7, 2, 6, 3, 5, 4)


def at(axis, step):
    return lax.rem(lax.axis_index(axis) + (step % SIZE[axis]), SIZE[axis])


def z_peer(p, sign):
    return {"z": at("z", sign * DZ[p // 2]), "c": at("c", p % 2)}


def xy_peer(j):
    return {"x": at("x", j // 4), "y": at("y", j % 4)}


def nt(a, b):
    return lax.dot_general(a, b, (((1,), (1,)), ((), ())), preferred_element_type=F32)


def nn(a, b):
    return jnp.dot(a, b, preferred_element_type=F32)


class RingGather:
    def __init__(self, buf, send, recv):
        self.buf, self.send, self.recv = buf, send, recv
        self.copies = {}

    def go(self, number, view, peer):
        c = pltpu.make_async_remote_copy(
            src_ref=view, dst_ref=view, send_sem=self.send.at[number], recv_sem=self.recv.at[number], device_id=peer
        )
        c.start()
        self.copies[number] = c

    def got(self, *numbers):
        for n in numbers:
            self.copies[n].wait_recv()

    def step(self, s):
        buf, h, q = self.buf, N // 2, N // 4
        x, y = lax.axis_index("x"), lax.axis_index("y")
        xl, xr, yl, yr = at("x", -1), at("x", 1), at("y", -1), at("y", 1)
        top, bot = pl.ds(0, h), pl.ds(h, h)
        parts = [pl.ds(i * q, q) for i in range(4)]
        if s == 0:
            self.go(0, buf.at[x, y, top], {"x": xr})
            self.go(1, buf.at[x, y, top], {"x": xl})
            self.go(2, buf.at[x, y, bot], {"y": yr})
            self.go(3, buf.at[x, y, bot], {"y": yl})
        elif s == 1:
            self.got(0, 1, 2, 3)
            self.go(4, buf.at[xl, y, parts[0]], {"x": xr})
            self.go(5, buf.at[xr, y, parts[1]], {"x": xl})
            self.go(6, buf.at[x, yl, parts[2]], {"y": yr})
            self.go(7, buf.at[x, yr, parts[3]], {"y": yl})
        elif s == 2:
            self.got(4, 5, 6, 7)
            self.go(8, buf.at[:, y, top], {"y": yr})
            self.go(9, buf.at[:, y, top], {"y": yl})
            self.go(10, buf.at[x, :, bot], {"x": xr})
            self.go(11, buf.at[x, :, bot], {"x": xl})
        elif s == 3:
            self.got(8, 9, 10, 11)
            self.go(12, buf.at[:, yl, parts[0]], {"y": yr})
            self.go(13, buf.at[:, yr, parts[1]], {"y": yl})
            self.go(14, buf.at[xl, :, parts[2]], {"x": xr})
            self.go(15, buf.at[xr, :, parts[3]], {"x": xl})
        else:
            self.got(12, 13, 14, 15)
            for c in self.copies.values():
                c.wait_send()


class Sends:
    def __init__(self):
        self.copies = {}

    def go(self, key, src, dst, send, recv, peer):
        c = pltpu.make_async_remote_copy(
            src_ref=src, dst_ref=dst, send_sem=send, recv_sem=recv, device_id=peer
        )
        c.start()
        self.copies[key] = c

    def got(self, *keys):
        for k in keys:
            self.copies[k].wait_recv()

    def done(self):
        for c in self.copies.values():
            c.wait_send()


def column(row):
    return jnp.transpose(jnp.broadcast_to(row, (8, row.shape[1])))[:, 0:1]


def kernel(
    feats, ids, w_in_hbm, w_out_hbm, queries, qw, pos, counts,
    loss_o, gq_o, gi_o, gwi_o, gwo_o,
    w_in, w_out, q_all, u_all, nrm, ulow, unit, invlen, gs, acc, lb, plr, plc,
    snd, rcv, outb, ret, gsnd, grcv, gnb, gnret,
    gp, act_t, x_t, gh, pin, pout, ra_in, ra_out, pa_in, pa_out, rb_in, rb_out,
    st_s, st_r, bc_s, bc_r, lg,
    loc_sem, a1s, a1r, a2s, a2r, a3s, a3r, a4s, a4r, qs, qr, us, ur, sts, str_, bcs, bcr, rs_s, rs_r,
):
    x, y, z, c = (lax.axis_index(a) for a in AXES)
    barrier = pltpu.get_barrier_semaphore()
    for p in range(1, GROUP):
        pl.semaphore_signal(barrier, inc=1, device_id=z_peer(p, 1))
    for j in range(1, GROUP):
        pl.semaphore_signal(barrier, inc=1, device_id=xy_peer(j))

    load_in = pltpu.make_async_copy(w_in_hbm, w_in, loc_sem.at[0])
    load_out = pltpu.make_async_copy(w_out_hbm, w_out, loc_sem.at[1])
    load_in.start()
    load_out.start()

    f = feats[...].astype(F32)
    r = lax.rsqrt(jnp.mean(f * f, axis=1, keepdims=True) + EPS)
    nrm[...] = (f * r).astype(BF)
    idr = ids[...]
    hot = lax.broadcasted_iota(jnp.int32, (EXPERTS, N), 0) == idr
    earlier = lax.broadcasted_iota(jnp.int32, (N, N), 0) < lax.broadcasted_iota(jnp.int32, (N, N), 1)
    before = nn(hot.astype(F32).astype(BF), earlier.astype(F32).astype(BF))
    rank = jnp.sum(jnp.where(hot, before, 0.0), axis=0, keepdims=True).astype(jnp.int32)
    owner = idr >> 2
    dz = ((owner >> 1) - z) & 7
    dc = ((owner & 1) - c) & 1
    pz = jnp.where(dz <= 4, jnp.maximum(2 * dz - 1, 0), 16 - 2 * dz)
    local = idr & 3
    place = (local // EG) * GSLOTS + (pz * 2 + dc) * MSG + (local % EG) * CAP + rank
    plr[...] = place
    plc[...] = jnp.broadcast_to(column(place.astype(F32)).astype(jnp.int32), (N, D))

    def packed(values, g, i):
        slot = lax.broadcasted_iota(jnp.int32, (PACK, N), 0) + (g * GSLOTS + i * PACK)
        pick = (slot == plr[...]).astype(F32).astype(BF)
        return nn(pick, values[...]).astype(BF).reshape(PACK // MSG, EG, CAP, D)

    def unpacked(source, g):
        total = None
        for i in range(GSLOTS // D):
            slot = lax.broadcasted_iota(jnp.int32, (N, D), 1) + (g * GSLOTS + i * D)
            pick = (slot == plc[...]).astype(F32).astype(BF)
            n = D // MSG
            part = nn(pick, source[g, pl.ds(i * n, n)].reshape(D, D))
            total = part if total is None else total + part
        return total

    chunks = [(g, i) for g in range(NG) for i in reversed(range(GSLOTS // PACK))]
    n = PACK // MSG

    def pack(values, out, g, i):
        out[g, pl.ds(i * n, n)] = packed(values, g, i)

    def dispatch(sends, out, into, send, recv, g, i):
        for p in reversed(range(i * n, i * n + n)):
            if p:
                k = g * GROUP + p
                sends.go((g, p), out.at[g, p], into.at[g, p], send.at[k], recv.at[k], z_peer(p, 1))
        if i == 0:
            into[g, 0] = out[g, 0]

    def give_back(sends, out, into, send, recv, g):
        for p in reversed(range(1, GROUP)):
            k = g * GROUP + p
            sends.go((g, p), out.at[g, p], into.at[g, p], send.at[k], recv.at[k], z_peer(p, -1))
        into[g, 0] = out[g, 0]

    def group(g):
        return [(g, p) for p in range(1, GROUP)]

    gather_q = RingGather(q_all, qs, qr)
    gather_u = RingGather(u_all, us, ur)

    q_all[x, y] = queries[...]
    for g, i in chunks:
        pack(nrm, snd, g, i)
    pl.semaphore_wait(barrier, 2 * (GROUP - 1))
    sent1 = Sends()
    for g, i in chunks:
        dispatch(sent1, snd, rcv, a1s, a1r, g, i)
    gather_q.step(0)
    load_in.wait()
    load_out.wait()

    HALF = N // 2
    back2 = Sends()
    for g in range(NG):
        sent1.got(*group(g))

        def forward(k, _, g=g):
            e2, half = k // 2, lax.rem(k, 2)
            e = g * EG + e2
            rows = rcv[g, pl.ds(8 * half, 8), e2].reshape(HALF, D)
            h = nn(rows, w_in[e])
            gp[e, half] = h
            t = jnp.tanh(h * (K0 + K1 * (h * h)))
            act = (h * (0.5 + 0.5 * t)).astype(BF)
            out = nn(act, w_out[e]).astype(BF)
            outb[g, pl.ds(8 * half, 8), e2] = out.reshape(8, CAP, D)
            return _

        lax.fori_loop(0, 2 * EG, forward, 0)
        give_back(back2, outb, ret, a2s, a2r, g)
        gather_q.step(1 + g)
    for s in range(1 + NG, 4):
        gather_q.step(s)

    def keep(e, _):
        for half in range(2):
            for q in range(2):
                span = pl.ds(q * 128, 128)
                cols = pl.ds(half * HALF + q * 128, 128)
                h = gp[e, half, span]
                u = h * h
                t = jnp.tanh(h * (K0 + K1 * u))
                cdf = 0.5 + 0.5 * t
                gp[e, half, span] = cdf + (0.5 * h) * (1.0 - t * t) * (K0 + (3.0 * K1) * u)
                act_t[e, :, cols] = (h * cdf).astype(BF).T
        return _

    lax.fori_loop(0, NE, keep, 0)
    for e in range(NE):
        x_t[e] = rcv[e // EG, :, e % EG].reshape(N, D).T

    logc = jnp.log(counts[...].astype(F32))
    for d in range(GROUP):
        lg[d] = logc[:, d * N : (d + 1) * N]
    own_logc = column(lg[x * 4 + y])
    lb[...] = jnp.broadcast_to(own_logc, (N, T))

    for g in range(NG):
        back2.got(*group(g))
        if g == 0:
            acc[...] = unpacked(ret, g)
        else:
            acc[...] += unpacked(ret, g)

    summed = feats[...].astype(F32) + acc[...]
    length = jnp.sqrt(jnp.sum(summed * summed, axis=1, keepdims=True) + EPS)
    inv = 1.0 / length
    un = summed * inv
    unit[...] = un
    invlen[...] = jnp.broadcast_to(inv, (N, 128))
    ulow[...] = un.astype(BF)
    u_all[x, y] = un.astype(BF)
    gather_u.step(0)
    gather_q.step(4)

    def scores(qx, qy, t):
        return nt(ulow[...], q_all[qx, qy, pl.ds(t * T, T)]) - lb[...]

    def stat_block(j, _):
        qx, qy = lax.rem(x + j // 4, 4), lax.rem(y + lax.rem(j, 4), 4)
        for t in range(N // T):
            s = scores(qx, qy, t)
            m = jnp.max(s, axis=0, keepdims=True)
            st_s[j, 0:1, pl.ds(t * T, T)] = m
            st_s[j, 1:2, pl.ds(t * T, T)] = jnp.sum(jnp.exp(s - m), axis=0, keepdims=True)
        return _

    stats = Sends()
    for part in range(4):
        lax.fori_loop(4 * part, 4 * part + 4, stat_block, 0)
        for j in range(4 * part, 4 * part + 4):
            if j:
                stats.go(j, st_s.at[j], st_r.at[j], sts.at[j], str_.at[j], xy_peer(j))
    st_r[0] = st_s[0]
    gather_u.step(1)
    stats.got(*range(1, GROUP))
    top = jnp.max(st_r[:, 0:1, :], axis=0)
    total = jnp.sum(st_r[:, 1:2, :] * jnp.exp(st_r[:, 0:1, :] - top[None]), axis=0)
    lse = top + jnp.log(total)
    bc_s[0:1] = lse - jnp.log(qw[...])
    bc_s[1:2] = qw[...]
    bc_s[2:3] = pos[...].astype(F32)
    bc_s[3:4] = lse
    shared = Sends()
    for j in range(1, GROUP):
        shared.go(j, bc_s, bc_r.at[j], bcs.at[j], bcr.at[j], xy_peer(j))
    bc_r[0] = bc_s[...]
    gather_u.step(2)
    first_item = ((x * 4 + y) * N).astype(F32)

    acc[...] = jnp.zeros((N, D), F32)
    item_row = lax.broadcasted_iota(jnp.int32, (N, T), 0)

    def grad_block(j, _):
        qx, qy = lax.rem(x + 4 - j // 4, 4), lax.rem(y + 4 - lax.rem(j, 4), 4)
        for t in range(N // T):
            span = pl.ds(t * T, T)
            s = scores(qx, qy, t)
            e = jnp.exp(s - bc_r[j, 0:1, span])
            own = (bc_r[j, 2:3, span] - first_item).astype(jnp.int32)
            coeff = (e - jnp.where(item_row == own, bc_r[j, 1:2, span], 0.0)).astype(BF)
            acc[...] += nn(coeff, q_all[qx, qy, span])
        return _

    for part in range(4):
        shared.got(*range(max(1, 4 * part), 4 * part + 4))
        lax.fori_loop(4 * part, 4 * part + 4, grad_block, 0)
        if part == 2:
            gather_u.step(3)

    g_unit = acc[...]
    un = unit[...]
    along = jnp.sum(un * g_unit, axis=1, keepdims=True)
    gsum = (g_unit - un * along) * invlen[:, 0:1]
    gs[...] = gsum
    nrm[...] = gsum.astype(BF)
    sent3 = Sends()
    for g, i in chunks:
        pack(nrm, gsnd, g, i)
        dispatch(sent3, gsnd, grcv, a3s, a3r, g, i)

    gather_u.step(4)
    acc[...] = jnp.zeros((N, D), F32)
    lse_c = column(lse)
    weight_c = column(qw[...])
    lb[...] = jnp.broadcast_to(lse_c - jnp.log(weight_c), (N, T))
    plq = jnp.broadcast_to(column(pos[...].astype(F32)).astype(jnp.int32), (N, 128))
    weight_b = jnp.broadcast_to(weight_c, (N, 128))
    invlen[...] = jnp.zeros((N, 128), F32)

    def query_block(d, _):
        ix, iy = d // 4, lax.rem(d, 4)
        for t in range(N // 128):
            span = pl.ds(t * 128, 128)
            s = nt(queries[...], u_all[ix, iy, span]) - lg[d, :, span]
            e = jnp.exp(s - lb[:, 0:128])
            hit = lax.broadcasted_iota(jnp.int32, (N, 128), 1) + (d * N + t * 128) == plq
            coeff = (e - jnp.where(hit, weight_b, 0.0)).astype(BF)
            invlen[...] += jnp.where(hit, s, 0.0)
            acc[...] += nn(coeff, u_all[ix, iy, span])
        return _

    lax.fori_loop(0, QCUT, query_block, 0)

    back4 = Sends()
    rs = Sends()

    def reduce_go(g, number, src, dst, peer):
        rs.go((g, number), src, dst, rs_s.at[g * 12 + number], rs_r.at[g * 12 + number], peer)

    for g in range(NG):
        sent3.got(*group(g))

        def backward(k, _, g=g):
            e2, half = k // 2, lax.rem(k, 2)
            e = g * EG + e2
            rows = grcv[g, pl.ds(8 * half, 8), e2].reshape(HALF, D)
            ghv = (nt(rows, w_out[e]) * gp[e, half]).astype(BF)
            gh[e, half] = ghv
            gnb[g, pl.ds(8 * half, 8), e2] = nt(ghv, w_in[e]).astype(BF).reshape(8, CAP, D)
            return _

        lax.fori_loop(0, 2 * EG, backward, 0)
        give_back(back4, gnb, gnret, a4s, a4r, g)

        def weights(e2, _, g=g):
            e = g * EG + e2
            pin[g, :, :, e2] = nn(x_t[e], gh[e].reshape(N, FF)).astype(BF).reshape(4, 4, 16, FF)
            rows = grcv[g, :, e2].reshape(N, D)
            pout[g, :, :, e2] = nn(act_t[e], rows).astype(BF).reshape(4, 4, 64, D)
            return _

        lax.fori_loop(0, EG, weights, 0)
        for k in (1, 3, 2):
            reduce_go(g, k - 1, pin.at[g, at("x", k)], ra_in.at[g, k - 1], {"x": at("x", k)})
            reduce_go(g, k + 2, pout.at[g, :, at("y", k)], ra_out.at[g, k - 1], {"y": at("y", k)})
    lax.fori_loop(QCUT, GROUP, query_block, 0)
    gq_o[...] = acc[...]
    picked = jnp.sum(invlen[...], axis=1, keepdims=True)
    loss_o[...] = jnp.transpose(jnp.broadcast_to(lse_c - picked, (N, 128)))[0:1]

    def first_sums(g):
        rs.got(*[(g, n) for n in range(6)])
        for k in range(4):
            t = pin[g, x, k].astype(F32)
            u = pout[g, k, y].astype(F32)
            for i in range(3):
                t = t + ra_in[g, i, k].astype(F32)
                u = u + ra_out[g, i, k].astype(F32)
            pa_in[g, k] = t.astype(BF)
            pa_out[g, k] = u.astype(BF)
        for k in (1, 3, 2):
            reduce_go(g, k + 5, pa_in.at[g, at("y", k)], rb_in.at[g, k - 1], {"y": at("y", k)})
            reduce_go(g, k + 8, pa_out.at[g, at("x", k)], rb_out.at[g, k - 1], {"x": at("x", k)})

    def last_sums(g):
        rs.got(*[(g, n) for n in range(6, 12)])
        t = pa_in[g, y].astype(F32)
        u = pa_out[g, x].astype(F32)
        for i in range(3):
            t = t + rb_in[g, i].astype(F32)
            u = u + rb_out[g, i].astype(F32)
        gwi_o[pl.ds(g * EG, EG)] = t
        gwo_o[pl.ds(g * EG, EG)] = u

    for g in range(NG):
        first_sums(g)
    for g in range(NG):
        back4.got(*group(g))
        if g == 0:
            acc[...] = unpacked(gnret, g)
        else:
            acc[...] += unpacked(gnret, g)
        if g < NG - 1:
            last_sums(g)
    f = feats[...].astype(F32)
    r = lax.rsqrt(jnp.mean(f * f, axis=1, keepdims=True) + EPS)
    grows = acc[...]
    projected = jnp.mean(grows * f, axis=1, keepdims=True)
    gi_o[...] = gs[...] + r * (grows - f * (r * r * projected))
    last_sums(NG - 1)
    for sends in (sent1, back2, stats, shared, sent3, back4, rs):
        sends.done()


def finishing(loss, gq, gi, gwi, gwo, loss_o, gq_o, gi_o, gwi_o, gwo_o):
    loss_o[...] = loss[...]
    gq_o[...] = gq[...]
    gi_o[...] = gi[...]
    for e in range(NE):
        gwi_o[:, e, :] = gwi[e]
        gwo_o[:, e, :] = gwo[e]


def per_device(feats, ids, w_in, w_out, queries, qw, pos, counts):
    vm = pl.BlockSpec(memory_space=pltpu.VMEM)
    hbm = pl.BlockSpec(memory_space=pl.ANY)
    V = pltpu.VMEM
    sem = pltpu.SemaphoreType.DMA
    slots = (NG, GROUP, EG, CAP, D)
    many = sem((NG * GROUP,))
    scratch = [
        V((NE, D, FF), BF), V((NE, FF, D), BF), V((4, 4, N, D), BF), V((4, 4, N, D), BF),
        V((N, D), BF), V((N, D), BF), V((N, D), F32), V((N, 128), F32), V((N, D), F32), V((N, D), F32), V((N, T), F32),
        V((1, N), jnp.int32), V((N, D), jnp.int32),
        *[V(slots, BF) for _ in range(8)],
        V((NE, 2, N // 2, FF), F32), V((NE, FF, N), BF), V((NE, D, N), BF), V((NE, 2, N // 2, FF), BF),
        V((NG, 4, 4, EG, 16, FF), BF), V((NG, 4, 4, EG, 64, D), BF),
        V((NG, 3, 4, EG, 16, FF), BF), V((NG, 3, 4, EG, 64, D), BF),
        V((NG, 4, EG, 16, FF), BF), V((NG, 4, EG, 64, D), BF),
        V((NG, 3, EG, 16, FF), BF), V((NG, 3, EG, 64, D), BF),
        V((GROUP, 2, N), F32), V((GROUP, 2, N), F32), V((4, N), F32), V((GROUP, 4, N), F32), V((GROUP, 1, N), F32),
        sem((2,)), *[many for _ in range(8)], *[sem((GROUP,)) for _ in range(8)], sem((NG * 12,)), sem((NG * 12,)),
    ]
    made = (
        jax.ShapeDtypeStruct((1, N), F32),
        jax.ShapeDtypeStruct((N, D), F32),
        jax.ShapeDtypeStruct((N, D), F32),
        jax.ShapeDtypeStruct((NE, 16, FF), F32),
        jax.ShapeDtypeStruct((NE, 64, D), F32),
    )
    results = pl.pallas_call(
        kernel,
        out_shape=made,
        in_specs=[vm, vm, hbm, hbm, vm, vm, vm, vm],
        out_specs=[vm] * 5,
        scratch_shapes=scratch,
        compiler_params=pltpu.CompilerParams(
            collective_id=0, has_side_effects=True, vmem_limit_bytes=60 << 20
        ),
        name="tower_step",
    )(feats[0], ids.reshape(1, N), w_in, w_out, queries[0], qw, pos, counts)
    outs = (*made[:3], jax.ShapeDtypeStruct((16, NE, FF), F32), jax.ShapeDtypeStruct((64, NE, D), F32))
    loss, gq, gi, gwi, gwo = pl.pallas_call(
        finishing, out_shape=outs, in_specs=[vm] * 5, out_specs=[vm] * 5, name="write_out"
    )(*results)
    return (loss, gq[None], gi[None], gwi, gwo)


def solution(mesh):
    torus = Mesh(mesh.devices.reshape(4, 4, 8, 2), AXES)
    dp, ex = ("x", "y"), ("z", "c")
    in_specs = (
        P(ex, dp, None), P(ex, dp, None), P(ex, None, None), P(ex, None, None),
        P(ex, dp, None), P(ex, dp), P(ex, dp), P(ex, None),
    )
    out_specs = (
        P(ex, dp), P(ex, dp, None), P(ex, dp, None), P(dp, ex, None), P(dp, ex, None),
    )
    return jax.shard_map(
        per_device, mesh=torus, in_specs=in_specs, out_specs=out_specs, check_vma=False
    )
```

```python
import functools
import math

import jax
import jax.numpy as jnp
from jax import lax
from jax.experimental import pallas as pl
from jax.experimental.pallas import tpu as pltpu
from jax.sharding import Mesh
from jax.sharding import PartitionSpec as P

AXES = ("x", "y", "z", "c")
SIZE = {"x": 4, "y": 4, "z": 8, "c": 2}
N = 512
D = 256
FF = 1024
NE = 4
CAP = 32
EXPERTS = 64
GROUP = 16
SLOTS = NE * CAP
NG = 2
EG = NE // NG
MSG = EG * CAP
GSLOTS = GROUP * MSG
T = 256
QCUT = 8
PACK = 512
EPS = 1e-6
K0 = math.sqrt(2.0 / math.pi)
K1 = K0 * 0.044715
BF = jnp.bfloat16
F32 = jnp.float32

DZ = (0, 1, 7, 2, 6, 3, 5, 4)


def at(axis, step):
    return lax.rem(lax.axis_index(axis) + (step % SIZE[axis]), SIZE[axis])


def z_peer(p, sign):
    return {"z": at("z", sign * DZ[p // 2]), "c": at("c", p % 2)}


def xy_peer(j):
    return {"x": at("x", j // 4), "y": at("y", j % 4)}


def nt(a, b):
    return lax.dot_general(a, b, (((1,), (1,)), ((), ())), preferred_element_type=F32)


def nn(a, b):
    return jnp.dot(a, b, preferred_element_type=F32)


class RingGather:
    def __init__(self, buf, send, recv):
        self.buf, self.send, self.recv = buf, send, recv
        self.copies = {}

    def go(self, number, view, peer):
        c = pltpu.make_async_remote_copy(
            src_ref=view, dst_ref=view, send_sem=self.send.at[number], recv_sem=self.recv.at[number], device_id=peer
        )
        c.start()
        self.copies[number] = c

    def got(self, *numbers):
        for n in numbers:
            self.copies[n].wait_recv()

    def step(self, s):
        buf, h, q = self.buf, N // 2, N // 4
        x, y = lax.axis_index("x"), lax.axis_index("y")
        xl, xr, yl, yr = at("x", -1), at("x", 1), at("y", -1), at("y", 1)
        top, bot = pl.ds(0, h), pl.ds(h, h)
        parts = [pl.ds(i * q, q) for i in range(4)]
        if s == 0:
            self.go(0, buf.at[x, y, top], {"x": xr})
            self.go(1, buf.at[x, y, top], {"x": xl})
            self.go(2, buf.at[x, y, bot], {"y": yr})
            self.go(3, buf.at[x, y, bot], {"y": yl})
        elif s == 1:
            self.got(0, 1, 2, 3)
            self.go(4, buf.at[xl, y, parts[0]], {"x": xr})
            self.go(5, buf.at[xr, y, parts[1]], {"x": xl})
            self.go(6, buf.at[x, yl, parts[2]], {"y": yr})
            self.go(7, buf.at[x, yr, parts[3]], {"y": yl})
        elif s == 2:
            self.got(4, 5, 6, 7)
            self.go(8, buf.at[:, y, top], {"y": yr})
            self.go(9, buf.at[:, y, top], {"y": yl})
            self.go(10, buf.at[x, :, bot], {"x": xr})
            self.go(11, buf.at[x, :, bot], {"x": xl})
        elif s == 3:
            self.got(8, 9, 10, 11)
            self.go(12, buf.at[:, yl, parts[0]], {"y": yr})
            self.go(13, buf.at[:, yr, parts[1]], {"y": yl})
            self.go(14, buf.at[xl, :, parts[2]], {"x": xr})
            self.go(15, buf.at[xr, :, parts[3]], {"x": xl})
        else:
            self.got(12, 13, 14, 15)
            for c in self.copies.values():
                c.wait_send()


class Sends:
    def __init__(self):
        self.copies = {}

    def go(self, key, src, dst, send, recv, peer):
        c = pltpu.make_async_remote_copy(
            src_ref=src, dst_ref=dst, send_sem=send, recv_sem=recv, device_id=peer
        )
        c.start()
        self.copies[key] = c

    def got(self, *keys):
        for k in keys:
            self.copies[k].wait_recv()

    def done(self):
        for c in self.copies.values():
            c.wait_send()


def column(row):
    return jnp.transpose(jnp.broadcast_to(row, (8, row.shape[1])))[:, 0:1]


def kernel(
    feats, ids, w_in_hbm, w_out_hbm, queries, qw, pos, counts,
    loss_o, gq_o, gi_o, gwi_o, gwo_o,
    w_in, w_out, q_all, u_all, nrm, ulow, unit, invlen, gs, acc, lb, plr, plc,
    snd, rcv, outb, ret, gsnd, grcv, gnb, gnret,
    gp, act_t, x_t, gh, pin, pout, ra_in, ra_out, pa_in, pa_out, rb_in, rb_out,
    st_s, st_r, bc_s, bc_r, lg,
    loc_sem, a1s, a1r, a2s, a2r, a3s, a3r, a4s, a4r, qs, qr, us, ur, sts, str_, bcs, bcr, rs_s, rs_r,
):
    x, y, z, c = (lax.axis_index(a) for a in AXES)
    barrier = pltpu.get_barrier_semaphore()
    for p in range(1, GROUP):
        pl.semaphore_signal(barrier, inc=1, device_id=z_peer(p, 1))
    for j in range(1, GROUP):
        pl.semaphore_signal(barrier, inc=1, device_id=xy_peer(j))

    load_in = pltpu.make_async_copy(w_in_hbm, w_in, loc_sem.at[0])
    load_out = pltpu.make_async_copy(w_out_hbm, w_out, loc_sem.at[1])
    load_in.start()
    load_out.start()

    f = feats[...].astype(F32)
    r = lax.rsqrt(jnp.mean(f * f, axis=1, keepdims=True) + EPS)
    nrm[...] = (f * r).astype(BF)
    idr = ids[...]
    hot = lax.broadcasted_iota(jnp.int32, (EXPERTS, N), 0) == idr
    earlier = lax.broadcasted_iota(jnp.int32, (N, N), 0) < lax.broadcasted_iota(jnp.int32, (N, N), 1)
    before = nn(hot.astype(F32).astype(BF), earlier.astype(F32).astype(BF))
    rank = jnp.sum(jnp.where(hot, before, 0.0), axis=0, keepdims=True).astype(jnp.int32)
    owner = idr >> 2
    dz = ((owner >> 1) - z) & 7
    dc = ((owner & 1) - c) & 1
    pz = jnp.where(dz <= 4, jnp.maximum(2 * dz - 1, 0), 16 - 2 * dz)
    local = idr & 3
    place = (local // EG) * GSLOTS + (pz * 2 + dc) * MSG + (local % EG) * CAP + rank
    plr[...] = place
    plc[...] = jnp.broadcast_to(column(place.astype(F32)).astype(jnp.int32), (N, D))

    def packed(values, g, i):
        slot = lax.broadcasted_iota(jnp.int32, (PACK, N), 0) + (g * GSLOTS + i * PACK)
        pick = (slot == plr[...]).astype(F32).astype(BF)
        return nn(pick, values[...]).astype(BF).reshape(PACK // MSG, EG, CAP, D)

    def unpacked(source, g):
        total = None
        for i in range(GSLOTS // D):
            slot = lax.broadcasted_iota(jnp.int32, (N, D), 1) + (g * GSLOTS + i * D)
            pick = (slot == plc[...]).astype(F32).astype(BF)
            n = D // MSG
            part = nn(pick, source[g, pl.ds(i * n, n)].reshape(D, D))
            total = part if total is None else total + part
        return total

    chunks = [(g, i) for g in range(NG) for i in reversed(range(GSLOTS // PACK))]
    n = PACK // MSG

    def pack(values, out, g, i):
        out[g, pl.ds(i * n, n)] = packed(values, g, i)

    def dispatch(sends, out, into, send, recv, g, i):
        for p in reversed(range(i * n, i * n + n)):
            if p:
                k = g * GROUP + p
                sends.go((g, p), out.at[g, p], into.at[g, p], send.at[k], recv.at[k], z_peer(p, 1))
        if i == 0:
            into[g, 0] = out[g, 0]

    def give_back(sends, out, into, send, recv, g):
        for p in reversed(range(1, GROUP)):
            k = g * GROUP + p
            sends.go((g, p), out.at[g, p], into.at[g, p], send.at[k], recv.at[k], z_peer(p, -1))
        into[g, 0] = out[g, 0]

    def group(g):
        return [(g, p) for p in range(1, GROUP)]

    gather_q = RingGather(q_all, qs, qr)
    gather_u = RingGather(u_all, us, ur)

    q_all[x, y] = queries[...]
    for g, i in chunks:
        pack(nrm, snd, g, i)
    pl.semaphore_wait(barrier, 2 * (GROUP - 1))
    sent1 = Sends()
    for g, i in chunks:
        dispatch(sent1, snd, rcv, a1s, a1r, g, i)
    gather_q.step(0)
    load_in.wait()
    load_out.wait()

    HALF = N // 2
    back2 = Sends()
    for g in range(NG):
        sent1.got(*group(g))

        def forward(k, _, g=g):
            e2, half = k // 2, lax.rem(k, 2)
            e = g * EG + e2
            rows = rcv[g, pl.ds(8 * half, 8), e2].reshape(HALF, D)
            h = nn(rows, w_in[e])
            gp[e, half] = h
            t = jnp.tanh(h * (K0 + K1 * (h * h)))
            act = (h * (0.5 + 0.5 * t)).astype(BF)
            out = nn(act, w_out[e]).astype(BF)
            outb[g, pl.ds(8 * half, 8), e2] = out.reshape(8, CAP, D)
            return _

        lax.fori_loop(0, 2 * EG, forward, 0)
        give_back(back2, outb, ret, a2s, a2r, g)
        gather_q.step(1 + g)
    def keep(e, _):
        for half in range(2):
            for q in range(2):
                span = pl.ds(q * 128, 128)
                cols = pl.ds(half * HALF + q * 128, 128)
                h = gp[e, half, span]
                u = h * h
                t = jnp.tanh(h * (K0 + K1 * u))
                cdf = 0.5 + 0.5 * t
                gp[e, half, span] = cdf + (0.5 * h) * (1.0 - t * t) * (K0 + (3.0 * K1) * u)
                act_t[e, :, cols] = (h * cdf).astype(BF).T
        return _

    lax.fori_loop(0, NE, keep, 0)
    gather_q.step(3)
    for e in range(NE):
        x_t[e] = rcv[e // EG, :, e % EG].reshape(N, D).T

    logc = jnp.log(counts[...].astype(F32))
    for d in range(GROUP):
        lg[d] = logc[:, d * N : (d + 1) * N]
    own_logc = column(lg[x * 4 + y])
    lb[...] = jnp.broadcast_to(own_logc, (N, T))

    for g in range(NG):
        back2.got(*group(g))
        if g == 0:
            acc[...] = unpacked(ret, g)
        else:
            acc[...] += unpacked(ret, g)

    summed = feats[...].astype(F32) + acc[...]
    length = jnp.sqrt(jnp.sum(summed * summed, axis=1, keepdims=True) + EPS)
    inv = 1.0 / length
    un = summed * inv
    unit[...] = un
    invlen[...] = jnp.broadcast_to(inv, (N, 128))
    ulow[...] = un.astype(BF)
    u_all[x, y] = un.astype(BF)
    gather_u.step(0)
    gather_q.step(4)

    def scores(qx, qy, t):
        return nt(ulow[...], q_all[qx, qy, pl.ds(t * T, T)]) - lb[...]

    def stat_block(j, _):
        qx, qy = lax.rem(x + j // 4, 4), lax.rem(y + lax.rem(j, 4), 4)
        for t in range(N // T):
            s = scores(qx, qy, t)
            m = jnp.max(s, axis=0, keepdims=True)
            st_s[j, 0:1, pl.ds(t * T, T)] = m
            st_s[j, 1:2, pl.ds(t * T, T)] = jnp.sum(jnp.exp(s - m), axis=0, keepdims=True)
        return _

    stats = Sends()
    for part in range(4):
        lax.fori_loop(4 * part, 4 * part + 4, stat_block, 0, unroll=True)
        for j in range(4 * part, 4 * part + 4):
            if j:
                stats.go(j, st_s.at[j], st_r.at[j], sts.at[j], str_.at[j], xy_peer(j))
    st_r[0] = st_s[0]
    gather_u.step(1)
    stats.got(*range(1, GROUP))
    top = jnp.max(st_r[:, 0:1, :], axis=0)
    total = jnp.sum(st_r[:, 1:2, :] * jnp.exp(st_r[:, 0:1, :] - top[None]), axis=0)
    lse = top + jnp.log(total)
    bc_s[0:1] = lse - jnp.log(qw[...])
    bc_s[1:2] = qw[...]
    bc_s[2:3] = pos[...].astype(F32)
    bc_s[3:4] = lse
    shared = Sends()
    for j in range(1, GROUP):
        shared.go(j, bc_s, bc_r.at[j], bcs.at[j], bcr.at[j], xy_peer(j))
    bc_r[0] = bc_s[...]
    gather_u.step(2)
    first_item = ((x * 4 + y) * N).astype(F32)

    acc[...] = jnp.zeros((N, D), F32)
    item_row = lax.broadcasted_iota(jnp.int32, (N, T), 0)

    def grad_block(j, _):
        qx, qy = lax.rem(x + 4 - j // 4, 4), lax.rem(y + 4 - lax.rem(j, 4), 4)
        for t in range(N // T):
            span = pl.ds(t * T, T)
            s = scores(qx, qy, t)
            e = jnp.exp(s - bc_r[j, 0:1, span])
            own = (bc_r[j, 2:3, span] - first_item).astype(jnp.int32)
            coeff = (e - jnp.where(item_row == own, bc_r[j, 1:2, span], 0.0)).astype(BF)
            acc[...] += nn(coeff, q_all[qx, qy, span])
        return _

    for part in range(4):
        shared.got(*range(max(1, 4 * part), 4 * part + 4))
        lax.fori_loop(4 * part, 4 * part + 4, grad_block, 0, unroll=True)

    g_unit = acc[...]
    un = unit[...]
    along = jnp.sum(un * g_unit, axis=1, keepdims=True)
    gsum = (g_unit - un * along) * invlen[:, 0:1]
    gs[...] = gsum
    nrm[...] = gsum.astype(BF)
    sent3 = Sends()
    for g, i in chunks:
        pack(nrm, gsnd, g, i)
        dispatch(sent3, gsnd, grcv, a3s, a3r, g, i)

    gather_u.step(3)

    acc[...] = jnp.zeros((N, D), F32)
    lse_c = column(lse)
    weight_c = column(qw[...])
    lb[...] = jnp.broadcast_to(lse_c - jnp.log(weight_c), (N, T))
    plq = jnp.broadcast_to(column(pos[...].astype(F32)).astype(jnp.int32), (N, 128))
    weight_b = jnp.broadcast_to(weight_c, (N, 128))
    invlen[...] = jnp.zeros((N, 128), F32)

    def query_block(d, _):
        ix, iy = d // 4, lax.rem(d, 4)
        for t in range(N // 128):
            span = pl.ds(t * 128, 128)
            s = nt(queries[...], u_all[ix, iy, span]) - lg[d, :, span]
            e = jnp.exp(s - lb[:, 0:128])
            hit = lax.broadcasted_iota(jnp.int32, (N, 128), 1) + (d * N + t * 128) == plq
            coeff = (e - jnp.where(hit, weight_b, 0.0)).astype(BF)
            invlen[...] += jnp.where(hit, s, 0.0)
            acc[...] += nn(coeff, u_all[ix, iy, span])
        return _

    back4 = Sends()
    rs = Sends()

    def reduce_go(g, number, src, dst, peer):
        rs.go((g, number), src, dst, rs_s.at[g * 12 + number], rs_r.at[g * 12 + number], peer)

    for g in range(NG):
        sent3.got(*group(g))

        def backward(k, _, g=g):
            e2, half = k // 2, lax.rem(k, 2)
            e = g * EG + e2
            rows = grcv[g, pl.ds(8 * half, 8), e2].reshape(HALF, D)
            ghv = (nt(rows, w_out[e]) * gp[e, half]).astype(BF)
            gh[e, half] = ghv
            gnb[g, pl.ds(8 * half, 8), e2] = nt(ghv, w_in[e]).astype(BF).reshape(8, CAP, D)
            return _

        lax.fori_loop(0, 2 * EG, backward, 0)
        give_back(back4, gnb, gnret, a4s, a4r, g)

        def weights(e2, _, g=g):
            e = g * EG + e2
            pin[g, :, :, e2] = nn(x_t[e], gh[e].reshape(N, FF)).astype(BF).reshape(4, 4, 16, FF)
            rows = grcv[g, :, e2].reshape(N, D)
            pout[g, :, :, e2] = nn(act_t[e], rows).astype(BF).reshape(4, 4, 64, D)
            return _

        lax.fori_loop(0, EG, weights, 0)
        for k in (1, 3, 2):
            reduce_go(g, k - 1, pin.at[g, at("x", k)], ra_in.at[g, k - 1], {"x": at("x", k)})
            reduce_go(g, k + 2, pout.at[g, :, at("y", k)], ra_out.at[g, k - 1], {"y": at("y", k)})
        if g == 0:
            gather_u.step(4)
        lax.fori_loop(g * QCUT, (g + 1) * QCUT, query_block, 0)
    gq_o[...] = acc[...]
    picked = jnp.sum(invlen[...], axis=1, keepdims=True)
    loss_o[...] = jnp.transpose(jnp.broadcast_to(lse_c - picked, (N, 128)))[0:1]

    def first_sums(g):
        rs.got(*[(g, n) for n in range(6)])
        for k in range(4):
            t = pin[g, x, k].astype(F32)
            u = pout[g, k, y].astype(F32)
            for i in range(3):
                t = t + ra_in[g, i, k].astype(F32)
                u = u + ra_out[g, i, k].astype(F32)
            pa_in[g, k] = t.astype(BF)
            pa_out[g, k] = u.astype(BF)
        for k in (1, 3, 2):
            reduce_go(g, k + 5, pa_in.at[g, at("y", k)], rb_in.at[g, k - 1], {"y": at("y", k)})
            reduce_go(g, k + 8, pa_out.at[g, at("x", k)], rb_out.at[g, k - 1], {"x": at("x", k)})

    def last_sums(g):
        rs.got(*[(g, n) for n in range(6, 12)])
        t = pa_in[g, y].astype(F32)
        u = pa_out[g, x].astype(F32)
        for i in range(3):
            t = t + rb_in[g, i].astype(F32)
            u = u + rb_out[g, i].astype(F32)
        gwi_o[pl.ds(g * EG, EG)] = t
        gwo_o[pl.ds(g * EG, EG)] = u

    for g in range(NG):
        first_sums(g)
    for g in range(NG):
        back4.got(*group(g))
        if g == 0:
            acc[...] = unpacked(gnret, g)
        else:
            acc[...] += unpacked(gnret, g)
        if g < NG - 1:
            last_sums(g)
    f = feats[...].astype(F32)
    r = lax.rsqrt(jnp.mean(f * f, axis=1, keepdims=True) + EPS)
    grows = acc[...]
    projected = jnp.mean(grows * f, axis=1, keepdims=True)
    gi_o[...] = gs[...] + r * (grows - f * (r * r * projected))
    last_sums(NG - 1)
    for sends in (sent1, back2, stats, shared, sent3, back4, rs):
        sends.done()


def finishing(loss, gq, gi, gwi, gwo, loss_o, gq_o, gi_o, gwi_o, gwo_o):
    loss_o[...] = loss[...]
    gq_o[...] = gq[...]
    gi_o[...] = gi[...]
    for e in range(NE):
        gwi_o[:, e, :] = gwi[e]
        gwo_o[:, e, :] = gwo[e]


def per_device(feats, ids, w_in, w_out, queries, qw, pos, counts):
    vm = pl.BlockSpec(memory_space=pltpu.VMEM)
    hbm = pl.BlockSpec(memory_space=pl.ANY)
    V = pltpu.VMEM
    sem = pltpu.SemaphoreType.DMA
    slots = (NG, GROUP, EG, CAP, D)
    many = sem((NG * GROUP,))
    scratch = [
        V((NE, D, FF), BF), V((NE, FF, D), BF), V((4, 4, N, D), BF), V((4, 4, N, D), BF),
        V((N, D), BF), V((N, D), BF), V((N, D), F32), V((N, 128), F32), V((N, D), F32), V((N, D), F32), V((N, T), F32),
        V((1, N), jnp.int32), V((N, D), jnp.int32),
        *[V(slots, BF) for _ in range(8)],
        V((NE, 2, N // 2, FF), F32), V((NE, FF, N), BF), V((NE, D, N), BF), V((NE, 2, N // 2, FF), BF),
        V((NG, 4, 4, EG, 16, FF), BF), V((NG, 4, 4, EG, 64, D), BF),
        V((NG, 3, 4, EG, 16, FF), BF), V((NG, 3, 4, EG, 64, D), BF),
        V((NG, 4, EG, 16, FF), BF), V((NG, 4, EG, 64, D), BF),
        V((NG, 3, EG, 16, FF), BF), V((NG, 3, EG, 64, D), BF),
        V((GROUP, 2, N), F32), V((GROUP, 2, N), F32), V((4, N), F32), V((GROUP, 4, N), F32), V((GROUP, 1, N), F32),
        sem((2,)), *[many for _ in range(8)], *[sem((GROUP,)) for _ in range(8)], sem((NG * 12,)), sem((NG * 12,)),
    ]
    made = (
        jax.ShapeDtypeStruct((1, N), F32),
        jax.ShapeDtypeStruct((N, D), F32),
        jax.ShapeDtypeStruct((N, D), F32),
        jax.ShapeDtypeStruct((NE, 16, FF), F32),
        jax.ShapeDtypeStruct((NE, 64, D), F32),
    )
    results = pl.pallas_call(
        kernel,
        out_shape=made,
        in_specs=[vm, vm, hbm, hbm, vm, vm, vm, vm],
        out_specs=[vm] * 5,
        scratch_shapes=scratch,
        compiler_params=pltpu.CompilerParams(
            collective_id=0, has_side_effects=True, vmem_limit_bytes=60 << 20
        ),
        name="tower_step",
    )(feats[0], ids.reshape(1, N), w_in, w_out, queries[0], qw, pos, counts)
    outs = (*made[:3], jax.ShapeDtypeStruct((16, NE, FF), F32), jax.ShapeDtypeStruct((64, NE, D), F32))
    loss, gq, gi, gwi, gwo = pl.pallas_call(
        finishing, out_shape=outs, in_specs=[vm] * 5, out_specs=[vm] * 5, name="write_out"
    )(*results)
    return (loss, gq[None], gi[None], gwi, gwo)


def solution(mesh):
    torus = Mesh(mesh.devices.reshape(4, 4, 8, 2), AXES)
    dp, ex = ("x", "y"), ("z", "c")
    in_specs = (
        P(ex, dp, None), P(ex, dp, None), P(ex, None, None), P(ex, None, None),
        P(ex, dp, None), P(ex, dp), P(ex, dp), P(ex, None),
    )
    out_specs = (
        P(ex, dp), P(ex, dp, None), P(ex, dp, None), P(dp, ex, None), P(dp, ex, None),
    )
    return jax.shard_map(
        per_device, mesh=torus, in_specs=in_specs, out_specs=out_specs, check_vma=False
    )
```

```python
import functools
import math

import jax
import jax.numpy as jnp
from jax import lax
from jax.experimental import pallas as pl
from jax.experimental.pallas import tpu as pltpu
from jax.sharding import Mesh
from jax.sharding import PartitionSpec as P

AXES = ("x", "y", "z", "c")
SIZE = {"x": 4, "y": 4, "z": 8, "c": 2}
N = 512
D = 256
FF = 1024
NE = 4
CAP = 32
EXPERTS = 64
GROUP = 16
SLOTS = NE * CAP
NG = 2
EG = NE // NG
MSG = EG * CAP
GSLOTS = GROUP * MSG
T = 256
QCUT = (0, 4, 16)
PACK = 512
EPS = 1e-6
K0 = math.sqrt(2.0 / math.pi)
K1 = K0 * 0.044715
BF = jnp.bfloat16
F32 = jnp.float32

DZ = (0, 1, 7, 2, 6, 3, 5, 4)


def at(axis, step):
    return lax.rem(lax.axis_index(axis) + (step % SIZE[axis]), SIZE[axis])


def z_peer(p, sign):
    return {"z": at("z", sign * DZ[p // 2]), "c": at("c", p % 2)}


def xy_peer(j):
    return {"x": at("x", j // 4), "y": at("y", j % 4)}


def nt(a, b):
    return lax.dot_general(a, b, (((1,), (1,)), ((), ())), preferred_element_type=F32)


def nn(a, b):
    return jnp.dot(a, b, preferred_element_type=F32)


class RingGather:
    def __init__(self, buf, send, recv):
        self.buf, self.send, self.recv = buf, send, recv
        self.copies = {}

    def go(self, number, view, peer):
        c = pltpu.make_async_remote_copy(
            src_ref=view, dst_ref=view, send_sem=self.send.at[number], recv_sem=self.recv.at[number], device_id=peer
        )
        c.start()
        self.copies[number] = c

    def got(self, *numbers):
        for n in numbers:
            self.copies[n].wait_recv()

    def step(self, s):
        buf, h, q = self.buf, N // 2, N // 4
        x, y = lax.axis_index("x"), lax.axis_index("y")
        xl, xr, yl, yr = at("x", -1), at("x", 1), at("y", -1), at("y", 1)
        top, bot = pl.ds(0, h), pl.ds(h, h)
        parts = [pl.ds(i * q, q) for i in range(4)]
        if s == 0:
            self.go(0, buf.at[x, y, top], {"x": xr})
            self.go(1, buf.at[x, y, top], {"x": xl})
            self.go(2, buf.at[x, y, bot], {"y": yr})
            self.go(3, buf.at[x, y, bot], {"y": yl})
        elif s == 1:
            self.got(0, 1, 2, 3)
            self.go(4, buf.at[xl, y, parts[0]], {"x": xr})
            self.go(5, buf.at[xr, y, parts[1]], {"x": xl})
            self.go(6, buf.at[x, yl, parts[2]], {"y": yr})
            self.go(7, buf.at[x, yr, parts[3]], {"y": yl})
        elif s == 2:
            self.got(4, 5, 6, 7)
            self.go(8, buf.at[:, y, top], {"y": yr})
            self.go(9, buf.at[:, y, top], {"y": yl})
            self.go(10, buf.at[x, :, bot], {"x": xr})
            self.go(11, buf.at[x, :, bot], {"x": xl})
        elif s == 3:
            self.got(8, 9, 10, 11)
            self.go(12, buf.at[:, yl, parts[0]], {"y": yr})
            self.go(13, buf.at[:, yr, parts[1]], {"y": yl})
            self.go(14, buf.at[xl, :, parts[2]], {"x": xr})
            self.go(15, buf.at[xr, :, parts[3]], {"x": xl})
        else:
            self.got(12, 13, 14, 15)
            for c in self.copies.values():
                c.wait_send()


class Sends:
    def __init__(self):
        self.copies = {}

    def go(self, key, src, dst, send, recv, peer):
        c = pltpu.make_async_remote_copy(
            src_ref=src, dst_ref=dst, send_sem=send, recv_sem=recv, device_id=peer
        )
        c.start()
        self.copies[key] = c

    def got(self, *keys):
        for k in keys:
            self.copies[k].wait_recv()

    def done(self):
        for c in self.copies.values():
            c.wait_send()


def column(row):
    return jnp.transpose(jnp.broadcast_to(row, (8, row.shape[1])))[:, 0:1]


def kernel(
    feats, ids, w_in_hbm, w_out_hbm, queries, qw, pos, counts,
    loss_o, gq_o, gi_o, gwi_o, gwo_o,
    w_in, w_out, q_all, u_all, nrm, ulow, unit, invlen, gs, acc, lb, plr, plc,
    snd, rcv, outb, ret, gsnd, grcv, gnb, gnret,
    gp, act_t, x_t, gh, pin, pout, ra_in, ra_out, pa_in, pa_out, rb_in, rb_out,
    st_s, st_r, bc_s, bc_r, lg,
    loc_sem, a1s, a1r, a2s, a2r, a3s, a3r, a4s, a4r, qs, qr, us, ur, sts, str_, bcs, bcr, rs_s, rs_r,
):
    x, y, z, c = (lax.axis_index(a) for a in AXES)
    barrier = pltpu.get_barrier_semaphore()
    for p in range(1, GROUP):
        pl.semaphore_signal(barrier, inc=1, device_id=z_peer(p, 1))
    for j in range(1, GROUP):
        pl.semaphore_signal(barrier, inc=1, device_id=xy_peer(j))

    load_in = pltpu.make_async_copy(w_in_hbm, w_in, loc_sem.at[0])
    load_out = pltpu.make_async_copy(w_out_hbm, w_out, loc_sem.at[1])
    load_in.start()
    load_out.start()

    f = feats[...].astype(F32)
    r = lax.rsqrt(jnp.mean(f * f, axis=1, keepdims=True) + EPS)
    nrm[...] = (f * r).astype(BF)
    idr = ids[...]
    hot = lax.broadcasted_iota(jnp.int32, (EXPERTS, N), 0) == idr
    earlier = lax.broadcasted_iota(jnp.int32, (N, N), 0) < lax.broadcasted_iota(jnp.int32, (N, N), 1)
    before = nn(hot.astype(F32).astype(BF), earlier.astype(F32).astype(BF))
    rank = jnp.sum(jnp.where(hot, before, 0.0), axis=0, keepdims=True).astype(jnp.int32)
    owner = idr >> 2
    dz = ((owner >> 1) - z) & 7
    dc = ((owner & 1) - c) & 1
    pz = jnp.where(dz <= 4, jnp.maximum(2 * dz - 1, 0), 16 - 2 * dz)
    local = idr & 3
    place = (local // EG) * GSLOTS + (pz * 2 + dc) * MSG + (local % EG) * CAP + rank
    plr[...] = place
    plc[...] = jnp.broadcast_to(column(place.astype(F32)).astype(jnp.int32), (N, D))

    def packed(values, g, i):
        slot = lax.broadcasted_iota(jnp.int32, (PACK, N), 0) + (g * GSLOTS + i * PACK)
        pick = (slot == plr[...]).astype(F32).astype(BF)
        return nn(pick, values[...]).astype(BF).reshape(PACK // MSG, EG, CAP, D)

    def unpacked(source, g):
        total = None
        for i in range(GSLOTS // D):
            slot = lax.broadcasted_iota(jnp.int32, (N, D), 1) + (g * GSLOTS + i * D)
            pick = (slot == plc[...]).astype(F32).astype(BF)
            n = D // MSG
            part = nn(pick, source[g, pl.ds(i * n, n)].reshape(D, D))
            total = part if total is None else total + part
        return total

    chunks = [(g, i) for g in range(NG) for i in reversed(range(GSLOTS // PACK))]
    n = PACK // MSG

    def pack(values, out, g, i):
        out[g, pl.ds(i * n, n)] = packed(values, g, i)

    def dispatch(sends, out, into, send, recv, g, i):
        for p in reversed(range(i * n, i * n + n)):
            if p:
                k = g * GROUP + p
                sends.go((g, p), out.at[g, p], into.at[g, p], send.at[k], recv.at[k], z_peer(p, 1))
        if i == 0:
            into[g, 0] = out[g, 0]

    def give_back(sends, out, into, send, recv, g):
        for p in reversed(range(1, GROUP)):
            k = g * GROUP + p
            sends.go((g, p), out.at[g, p], into.at[g, p], send.at[k], recv.at[k], z_peer(p, -1))
        into[g, 0] = out[g, 0]

    def group(g):
        return [(g, p) for p in range(1, GROUP)]

    gather_q = RingGather(q_all, qs, qr)
    gather_u = RingGather(u_all, us, ur)

    q_all[x, y] = queries[...]
    for g, i in chunks:
        pack(nrm, snd, g, i)
    pl.semaphore_wait(barrier, 2 * (GROUP - 1))
    sent1 = Sends()
    for g, i in chunks:
        dispatch(sent1, snd, rcv, a1s, a1r, g, i)
    gather_q.step(0)
    load_in.wait()
    load_out.wait()

    HALF = N // 2
    back2 = Sends()
    for g in range(NG):
        sent1.got(*group(g))

        def forward(k, _, g=g):
            e2, half = k // 2, lax.rem(k, 2)
            e = g * EG + e2
            rows = rcv[g, pl.ds(8 * half, 8), e2].reshape(HALF, D)
            h = nn(rows, w_in[e])
            gp[e, half] = h
            t = jnp.tanh(h * (K0 + K1 * (h * h)))
            act = (h * (0.5 + 0.5 * t)).astype(BF)
            out = nn(act, w_out[e]).astype(BF)
            outb[g, pl.ds(8 * half, 8), e2] = out.reshape(8, CAP, D)
            return _

        lax.fori_loop(0, 2 * EG, forward, 0)
        give_back(back2, outb, ret, a2s, a2r, g)
        gather_q.step(1 + g)
    def keep(e, _):
        for half in range(2):
            for q in range(2):
                span = pl.ds(q * 128, 128)
                cols = pl.ds(half * HALF + q * 128, 128)
                h = gp[e, half, span]
                u = h * h
                t = jnp.tanh(h * (K0 + K1 * u))
                cdf = 0.5 + 0.5 * t
                gp[e, half, span] = cdf + (0.5 * h) * (1.0 - t * t) * (K0 + (3.0 * K1) * u)
                act_t[e, :, cols] = (h * cdf).astype(BF).T
        return _

    lax.fori_loop(0, NE, keep, 0)
    gather_q.step(3)
    for e in range(NE):
        x_t[e] = rcv[e // EG, :, e % EG].reshape(N, D).T

    logc = jnp.log(counts[...].astype(F32))
    for d in range(GROUP):
        lg[d] = logc[:, d * N : (d + 1) * N]
    own_logc = column(lg[x * 4 + y])
    lb[...] = jnp.broadcast_to(own_logc, (N, T))

    for g in range(NG):
        back2.got(*group(g))
        if g == 0:
            acc[...] = unpacked(ret, g)
        else:
            acc[...] += unpacked(ret, g)

    summed = feats[...].astype(F32) + acc[...]
    length = jnp.sqrt(jnp.sum(summed * summed, axis=1, keepdims=True) + EPS)
    inv = 1.0 / length
    un = summed * inv
    unit[...] = un
    invlen[...] = jnp.broadcast_to(inv, (N, 128))
    ulow[...] = un.astype(BF)
    u_all[x, y] = un.astype(BF)
    gather_u.step(0)
    gather_q.step(4)

    def scores(qx, qy, t):
        return nt(ulow[...], q_all[qx, qy, pl.ds(t * T, T)]) - lb[...]

    def stat_block(j, _):
        qx, qy = lax.rem(x + j // 4, 4), lax.rem(y + lax.rem(j, 4), 4)
        for t in range(N // T):
            s = scores(qx, qy, t)
            m = jnp.max(s, axis=0, keepdims=True)
            st_s[j, 0:1, pl.ds(t * T, T)] = m
            st_s[j, 1:2, pl.ds(t * T, T)] = jnp.sum(jnp.exp(s - m), axis=0, keepdims=True)
        return _

    stats = Sends()
    for part in range(4):
        lax.fori_loop(4 * part, 4 * part + 4, stat_block, 0, unroll=True)
        for j in range(4 * part, 4 * part + 4):
            if j:
                stats.go(j, st_s.at[j], st_r.at[j], sts.at[j], str_.at[j], xy_peer(j))
    st_r[0] = st_s[0]
    gather_u.step(1)
    stats.got(*range(1, GROUP))
    top = jnp.max(st_r[:, 0:1, :], axis=0)
    total = jnp.sum(st_r[:, 1:2, :] * jnp.exp(st_r[:, 0:1, :] - top[None]), axis=0)
    lse = top + jnp.log(total)
    bc_s[0:1] = lse - jnp.log(qw[...])
    bc_s[1:2] = qw[...]
    bc_s[2:3] = pos[...].astype(F32)
    bc_s[3:4] = lse
    shared = Sends()
    for j in range(1, GROUP):
        shared.go(j, bc_s, bc_r.at[j], bcs.at[j], bcr.at[j], xy_peer(j))
    bc_r[0] = bc_s[...]
    gather_u.step(2)
    first_item = ((x * 4 + y) * N).astype(F32)

    acc[...] = jnp.zeros((N, D), F32)
    item_row = lax.broadcasted_iota(jnp.int32, (N, T), 0)

    def grad_block(j, _):
        qx, qy = lax.rem(x + 4 - j // 4, 4), lax.rem(y + 4 - lax.rem(j, 4), 4)
        for t in range(N // T):
            span = pl.ds(t * T, T)
            s = scores(qx, qy, t)
            e = jnp.exp(s - bc_r[j, 0:1, span])
            own = (bc_r[j, 2:3, span] - first_item).astype(jnp.int32)
            coeff = (e - jnp.where(item_row == own, bc_r[j, 1:2, span], 0.0)).astype(BF)
            acc[...] += nn(coeff, q_all[qx, qy, span])
        return _

    for first, last in ((0, 1), (1, 4), (4, 8), (8, 12), (12, 16)):
        shared.got(*range(max(1, first), last))
        lax.fori_loop(first, last, grad_block, 0, unroll=True)

    g_unit = acc[...]
    un = unit[...]
    along = jnp.sum(un * g_unit, axis=1, keepdims=True)
    gsum = (g_unit - un * along) * invlen[:, 0:1]
    gs[...] = gsum
    nrm[...] = gsum.astype(BF)
    sent3 = Sends()
    for g, i in chunks:
        pack(nrm, gsnd, g, i)
        dispatch(sent3, gsnd, grcv, a3s, a3r, g, i)

    gather_u.step(3)

    acc[...] = jnp.zeros((N, D), F32)
    lse_c = column(lse)
    weight_c = column(qw[...])
    lb[...] = jnp.broadcast_to(lse_c - jnp.log(weight_c), (N, T))
    plq = jnp.broadcast_to(column(pos[...].astype(F32)).astype(jnp.int32), (N, 128))
    weight_b = jnp.broadcast_to(weight_c, (N, 128))
    invlen[...] = jnp.zeros((N, 128), F32)

    def query_block(d, _):
        ix, iy = d // 4, lax.rem(d, 4)
        for t in range(N // 128):
            span = pl.ds(t * 128, 128)
            s = nt(queries[...], u_all[ix, iy, span]) - lg[d, :, span]
            e = jnp.exp(s - lb[:, 0:128])
            hit = lax.broadcasted_iota(jnp.int32, (N, 128), 1) + (d * N + t * 128) == plq
            coeff = (e - jnp.where(hit, weight_b, 0.0)).astype(BF)
            invlen[...] += jnp.where(hit, s, 0.0)
            acc[...] += nn(coeff, u_all[ix, iy, span])
        return _

    back4 = Sends()
    rs = Sends()

    def reduce_go(g, number, src, dst, peer):
        rs.go((g, number), src, dst, rs_s.at[g * 12 + number], rs_r.at[g * 12 + number], peer)

    for g in range(NG):
        sent3.got(*group(g))

        def backward(k, _, g=g):
            e2, half = k // 2, lax.rem(k, 2)
            e = g * EG + e2
            rows = grcv[g, pl.ds(8 * half, 8), e2].reshape(HALF, D)
            ghv = (nt(rows, w_out[e]) * gp[e, half]).astype(BF)
            gh[e, half] = ghv
            gnb[g, pl.ds(8 * half, 8), e2] = nt(ghv, w_in[e]).astype(BF).reshape(8, CAP, D)
            return _

        lax.fori_loop(0, 2 * EG, backward, 0)
        give_back(back4, gnb, gnret, a4s, a4r, g)

        def weights(e2, _, g=g):
            e = g * EG + e2
            pin[g, :, :, e2] = nn(x_t[e], gh[e].reshape(N, FF)).astype(BF).reshape(4, 4, 16, FF)
            rows = grcv[g, :, e2].reshape(N, D)
            pout[g, :, :, e2] = nn(act_t[e], rows).astype(BF).reshape(4, 4, 64, D)
            return _

        lax.fori_loop(0, EG, weights, 0)
        for k in (1, 3, 2):
            reduce_go(g, k - 1, pin.at[g, at("x", k)], ra_in.at[g, k - 1], {"x": at("x", k)})
            reduce_go(g, k + 2, pout.at[g, :, at("y", k)], ra_out.at[g, k - 1], {"y": at("y", k)})
        if g == 0:
            gather_u.step(4)
        lax.fori_loop(QCUT[g], QCUT[g + 1], query_block, 0)
    gq_o[...] = acc[...]
    picked = jnp.sum(invlen[...], axis=1, keepdims=True)
    loss_o[...] = jnp.transpose(jnp.broadcast_to(lse_c - picked, (N, 128)))[0:1]

    def first_sums(g):
        rs.got(*[(g, n) for n in range(6)])
        for k in range(4):
            t = pin[g, x, k].astype(F32)
            u = pout[g, k, y].astype(F32)
            for i in range(3):
                t = t + ra_in[g, i, k].astype(F32)
                u = u + ra_out[g, i, k].astype(F32)
            pa_in[g, k] = t.astype(BF)
            pa_out[g, k] = u.astype(BF)
        for k in (1, 3, 2):
            reduce_go(g, k + 5, pa_in.at[g, at("y", k)], rb_in.at[g, k - 1], {"y": at("y", k)})
            reduce_go(g, k + 8, pa_out.at[g, at("x", k)], rb_out.at[g, k - 1], {"x": at("x", k)})

    def last_sums(g):
        rs.got(*[(g, n) for n in range(6, 12)])
        t = pa_in[g, y].astype(F32)
        u = pa_out[g, x].astype(F32)
        for i in range(3):
            t = t + rb_in[g, i].astype(F32)
            u = u + rb_out[g, i].astype(F32)
        gwi_o[pl.ds(g * EG, EG)] = t
        gwo_o[pl.ds(g * EG, EG)] = u

    for g in range(NG):
        first_sums(g)
    for g in range(NG):
        back4.got(*group(g))
        if g == 0:
            acc[...] = unpacked(gnret, g)
        else:
            acc[...] += unpacked(gnret, g)
        if g < NG - 1:
            last_sums(g)
    f = feats[...].astype(F32)
    r = lax.rsqrt(jnp.mean(f * f, axis=1, keepdims=True) + EPS)
    grows = acc[...]
    projected = jnp.mean(grows * f, axis=1, keepdims=True)
    gi_o[...] = gs[...] + r * (grows - f * (r * r * projected))
    last_sums(NG - 1)
    for sends in (sent1, back2, stats, shared, sent3, back4, rs):
        sends.done()


def finishing(loss, gq, gi, gwi, gwo, loss_o, gq_o, gi_o, gwi_o, gwo_o):
    loss_o[...] = loss[...]
    gq_o[...] = gq[...]
    gi_o[...] = gi[...]
    for e in range(NE):
        gwi_o[:, e, :] = gwi[e]
        gwo_o[:, e, :] = gwo[e]


def per_device(feats, ids, w_in, w_out, queries, qw, pos, counts):
    vm = pl.BlockSpec(memory_space=pltpu.VMEM)
    hbm = pl.BlockSpec(memory_space=pl.ANY)
    V = pltpu.VMEM
    sem = pltpu.SemaphoreType.DMA
    slots = (NG, GROUP, EG, CAP, D)
    many = sem((NG * GROUP,))
    scratch = [
        V((NE, D, FF), BF), V((NE, FF, D), BF), V((4, 4, N, D), BF), V((4, 4, N, D), BF),
        V((N, D), BF), V((N, D), BF), V((N, D), F32), V((N, 128), F32), V((N, D), F32), V((N, D), F32), V((N, T), F32),
        V((1, N), jnp.int32), V((N, D), jnp.int32),
        *[V(slots, BF) for _ in range(8)],
        V((NE, 2, N // 2, FF), F32), V((NE, FF, N), BF), V((NE, D, N), BF), V((NE, 2, N // 2, FF), BF),
        V((NG, 4, 4, EG, 16, FF), BF), V((NG, 4, 4, EG, 64, D), BF),
        V((NG, 3, 4, EG, 16, FF), BF), V((NG, 3, 4, EG, 64, D), BF),
        V((NG, 4, EG, 16, FF), BF), V((NG, 4, EG, 64, D), BF),
        V((NG, 3, EG, 16, FF), BF), V((NG, 3, EG, 64, D), BF),
        V((GROUP, 2, N), F32), V((GROUP, 2, N), F32), V((4, N), F32), V((GROUP, 4, N), F32), V((GROUP, 1, N), F32),
        sem((2,)), *[many for _ in range(8)], *[sem((GROUP,)) for _ in range(8)], sem((NG * 12,)), sem((NG * 12,)),
    ]
    made = (
        jax.ShapeDtypeStruct((1, N), F32),
        jax.ShapeDtypeStruct((N, D), F32),
        jax.ShapeDtypeStruct((N, D), F32),
        jax.ShapeDtypeStruct((NE, 16, FF), F32),
        jax.ShapeDtypeStruct((NE, 64, D), F32),
    )
    results = pl.pallas_call(
        kernel,
        out_shape=made,
        in_specs=[vm, vm, hbm, hbm, vm, vm, vm, vm],
        out_specs=[vm] * 5,
        scratch_shapes=scratch,
        compiler_params=pltpu.CompilerParams(
            collective_id=0, has_side_effects=True, vmem_limit_bytes=60 << 20
        ),
        name="tower_step",
    )(feats[0], ids.reshape(1, N), w_in, w_out, queries[0], qw, pos, counts)
    outs = (*made[:3], jax.ShapeDtypeStruct((16, NE, FF), F32), jax.ShapeDtypeStruct((64, NE, D), F32))
    loss, gq, gi, gwi, gwo = pl.pallas_call(
        finishing, out_shape=outs, in_specs=[vm] * 5, out_specs=[vm] * 5, name="write_out"
    )(*results)
    return (loss, gq[None], gi[None], gwi, gwo)


def solution(mesh):
    torus = Mesh(mesh.devices.reshape(4, 4, 8, 2), AXES)
    dp, ex = ("x", "y"), ("z", "c")
    in_specs = (
        P(ex, dp, None), P(ex, dp, None), P(ex, None, None), P(ex, None, None),
        P(ex, dp, None), P(ex, dp), P(ex, dp), P(ex, None),
    )
    out_specs = (
        P(ex, dp), P(ex, dp, None), P(ex, dp, None), P(dp, ex, None), P(dp, ex, None),
    )
    return jax.shard_map(
        per_device, mesh=torus, in_specs=in_specs, out_specs=out_specs, check_vma=False
    )
```
